256 devices in a mesh: narrow: 8 (over x, core), wide: 32 (over y, z).
Axes of the slice: x: 4, y: 4, z: 8, core: 2. Of those that a mesh axis runs over, the one named last changes fastest.
Arguments:
- start_block: bfloat16 [8, 32, 32, 3584], P('narrow', 'wide'), may hold values from -360 to 360
- weights: bfloat16 [8, 32, 28, 12, 128, 128], P('narrow', 'wide'), may hold values from 0.049804688 to 1
- pattern: int32 [8, 32, 28, 12], P('narrow', 'wide'), may hold values from 0 to 33, as said below
Outputs:
- filtered_basis: float32 [8, 32, 32, 3584], P('narrow', 'wide')
The draws below stay inside these ranges and needn't reach their ends.
Inputs may be any that keep to these rules, and one draw needn't show every extreme that they name: `pattern`: slot 0 of each row block names the block itself; slots below 9, and every slot of blocks from 24 on, name blocks of the own tile; the other slots of a rim block name block value - 28 of the facing neighbour's rim that faces it.
All inputs are finite; a program needn't handle non-finite values.
Results may differ from the reference program's by a relative error of at most 0.0031.
Values may be sent and summed in bfloat16 or wider, within the bound.
A program may use at most 64 MiB of HBM per device.

```python
import math
import jax
import jax.numpy as jnp
from jax import lax

NVEC = 32
BS = 128
K = 12
K_IN = 9
RIM = 6
BLK = 28
MAPR = 8
MAPC = 32
TILE_ROWS = 3584
NDOCS = 917504


def draw_start_block(key, part):
    key_base, key_rows, key_cols = jax.random.split(key, 3)
    shape = (MAPR, MAPC, NVEC, TILE_ROWS)
    tile_count = MAPR * MAPC
    position = jnp.arange(tile_count, dtype=jnp.float32).reshape(MAPR, MAPC, 1, 1)
    rising = 1.0 + 2.0 * position / max(tile_count - 1, 1)
    row_scale = jnp.exp(jax.random.uniform(key_rows, (MAPR, MAPC, 1, TILE_ROWS)) * math.log(10.0))
    col_scale = jnp.exp(jax.random.uniform(key_cols, (1, 1, NVEC, 1)) * math.log(10.0))
    base = jnp.clip(jax.random.normal(key_base, shape), -4.0, 4.0)
    return (0.3 * base * row_scale * col_scale * rising).astype(jnp.bfloat16)


def draw_pattern(key, part):
    key_inner, key_outer = jax.random.split(key, 2)
    inward = jax.random.randint(key_inner, (MAPR, MAPC, BLK, K), 0, BLK)
    outward = BLK + jax.random.randint(key_outer, (MAPR, MAPC, BLK, K), 0, RIM)
    block_ids = jnp.arange(BLK, dtype=jnp.int32).reshape(1, 1, BLK, 1)
    slot_ids = jnp.arange(K, dtype=jnp.int32).reshape(1, 1, 1, K)
    chosen = jnp.where((slot_ids >= K_IN) & (block_ids < 4 * RIM), outward, inward)
    chosen = jnp.where(slot_ids == 0, block_ids, chosen)
    return chosen.astype(jnp.int32)


def steps_of(rng, dims, cuts, low, largest):
    def one(axis_at, blocks):
        heights = jax.random.uniform(jax.random.fold_in(jax.random.fold_in(rng, 6), axis_at), (blocks,), jnp.float32, low / len(cuts), largest / len(cuts))
        return jnp.repeat(jnp.exp(heights), dims[axis_at] // blocks).reshape((-1,) + (1,) * (len(dims) - axis_at - 1))

    gain = one(*cuts[0])
    for cut in cuts[1:]:
        gain = gain * one(*cut)
    return gain


def setup_inputs(seed: int = 0) -> dict:
    key_of = jax.random.split(jax.random.key(seed), 4)
    start_block = draw_start_block(jax.random.fold_in(key_of[3], 71), 0)
    weights = jnp.clip(jnp.exp(math.log(1.0) - 2.9996462 * jax.random.uniform(key_of[1], (MAPR, MAPC, BLK, K, BS, BS), jnp.float32) ** steps_of(key_of[1], (MAPR, MAPC, BLK, K, BS, BS), ((0, 8), (1, 32)), -0.2, 0.2)), 0.049804688, 1.0).astype(jnp.bfloat16)
    pattern = draw_pattern(jax.random.fold_in(key_of[3], 71), 0)
    return {"start_block": start_block, "weights": weights, "pattern": pattern}


lower_edge = 0.3
center = (2.0 + lower_edge) / 2.0
half_width = (2.0 - lower_edge) / 2.0
highest = lax.Precision.HIGHEST
opposite_rim = (1, 0, 3, 2)

def shifted(array_in, axis_index, step_by):
    length = array_in.shape[axis_index]
    zero_rim = jnp.zeros_like(lax.slice_in_dim(array_in, 0, 1, axis=axis_index))
    if step_by > 0:
        return jnp.concatenate([zero_rim, lax.slice_in_dim(array_in, 0, length - 1, axis=axis_index)], axis=axis_index)
    return jnp.concatenate([lax.slice_in_dim(array_in, 1, length, axis=axis_index), zero_rim], axis=axis_index)

def rim_part(array_in, rim_index):
    return array_in[:, :, :, rim_index * RIM:(rim_index + 1) * RIM]

def tile_product(tile_inputs):
    weight_block, extended_values, target, values = tile_inputs
    weight_wide = weight_block.astype(jnp.float32)
    gathered = jnp.take(extended_values, target, axis=1).astype(jnp.float32)
    forward = jnp.einsum('bsrc,nbsc->nbr', weight_wide, gathered)
    transposed = jnp.einsum('bsrc,nbr->bsnc', weight_wide, values.astype(jnp.float32))
    selector = (target[:, :, None] == jnp.arange(BLK + 4 * RIM, dtype=jnp.int32)[None, None, :]).astype(jnp.float32)
    grouped = jnp.einsum('bse,bsnc->nec', selector, transposed, precision=highest)
    return (forward, grouped)

def affinity(values, weights, target):
    segments = [shifted(rim_part(values, opposite_rim[direction]), direction // 2, 1 - 2 * (direction % 2)) for direction in range(4)]
    extended_values = jnp.concatenate([values] + segments, axis=3)
    tile_count = MAPR * MAPC

    def flatten(array_in):
        return array_in.reshape((tile_count,) + array_in.shape[2:])
    forward, grouped = lax.map(tile_product, (flatten(weights), flatten(extended_values), flatten(target), flatten(values)))
    forward = forward.reshape((MAPR, MAPC) + forward.shape[1:])
    grouped = grouped.reshape((MAPR, MAPC) + grouped.shape[1:])
    own_part = grouped[:, :, :, :BLK]
    outgoing = lax.optimization_barrier(grouped[:, :, :, BLK:].astype(jnp.bfloat16)).astype(jnp.float32)
    rim_added = [shifted(rim_part(outgoing, opposite_rim[direction]), direction // 2, 1 - 2 * (direction % 2)) for direction in range(4)]
    interior = jnp.zeros((MAPR, MAPC, values.shape[2], BLK - 4 * RIM, BS), jnp.float32)
    back_terms = own_part + jnp.concatenate(rim_added + [interior], axis=3)
    return 0.5 * (forward + back_terms)

def reference(start_block, weights, pattern):
    block_ids = jnp.arange(BLK, dtype=jnp.int32).reshape(1, 1, BLK, 1)
    facing = jnp.minimum(block_ids // RIM, 3)
    target = jnp.where(pattern < BLK, pattern, BLK + facing * RIM + (pattern - BLK)).astype(jnp.int32)
    ones_block = jnp.ones((MAPR, MAPC, 1, BLK, BS), jnp.bfloat16)
    degree = affinity(ones_block, weights, target)
    inv_root = 1.0 / jnp.sqrt(degree)

    def laplace(vectors):
        scaled = (inv_root * vectors).astype(jnp.bfloat16)
        return vectors - inv_root * affinity(scaled, weights, target)
    initial = start_block.reshape(MAPR, MAPC, NVEC, BLK, BS).astype(jnp.float32)
    previous = initial
    current = (laplace(initial) - center * initial) / half_width
    for repeat in range(2):
        following = 2.0 * (laplace(current) - center * current) / half_width - previous
        previous, current = (current, following)
    gram = jnp.einsum('ijnbr,ijmbr->nm', current, current, precision=highest)
    factor = jnp.linalg.cholesky(gram)
    inverse = lax.linalg.triangular_solve(factor, jnp.eye(NVEC, dtype=jnp.float32), left_side=True, lower=True)
    flattened = jnp.transpose(current, (2, 0, 1, 3, 4)).reshape(NVEC, NDOCS)
    result_basis = jnp.dot(inverse, flattened, precision=highest) * math.sqrt(NDOCS)
    return jnp.transpose(result_basis.reshape(NVEC, MAPR, MAPC, TILE_ROWS), (1, 2, 0, 3))
```

```python
import math

import jax
import jax.numpy as jnp
import numpy as np
from jax import lax
from jax.experimental import pallas as pl
from jax.experimental.pallas import tpu as pltpu
from jax.sharding import PartitionSpec as P

f32 = jnp.float32
bf16 = jnp.bfloat16
i32 = jnp.int32
MESH = pl.DeviceIdType.MESH

NVEC = 32
BS = 128
K = 12
K_IN = 9
RIM = 6
BLK = 28
RIM_ROWS = 4 * RIM
LOWER = 0.3
CENTER = (2.0 + LOWER) / 2.0
HALF = (2.0 - LOWER) / 2.0
OPP = (1, 0, 3, 2)

N_OWN = RIM_ROWS * K_IN + (BLK - RIM_ROWS) * K
N_RIM = RIM_ROWS * (K - K_IN)
OWN_PAIRS = (N_OWN + BLK) // 2
RIM_PAIRS = (N_RIM // 4 + RIM) // 2
T_GROUPS = 2
Z_CHIPS = 8
Y_CHIPS = 4

O_OW = 0
O_OU = O_OW + 2 * OWN_PAIRS
O_RW = O_OU + 2 * OWN_PAIRS
O_RU = O_RW + 8 * RIM_PAIRS
O_OE = O_RU + 8 * RIM_PAIRS
O_RE = O_OE + BLK
O_PT = O_RE + RIM_ROWS
F_OF = 0
F_RF = F_OF + OWN_PAIRS
F_NE = F_RF + 4 * RIM_PAIRS


def own_index(b):
    return b * K_IN if b < RIM_ROWS else RIM_ROWS * K_IN + (b - RIM_ROWS) * K


def sorted_lists(target, segments, group, base, pairs_total):
    count = target.shape[0]
    seg = np.arange(segments)
    hot = (target[:, None] == jnp.asarray(seg, i32)[None, :]).astype(i32)
    cnt = hot.sum(0)
    pairs = (cnt + 1) // 2
    before = jnp.asarray((seg[:, None] < seg[None, :]) & (seg[:, None] // group == seg[None, :] // group), i32)
    start = jnp.asarray(base, i32) + (pairs[:, None] * before).sum(0)
    order = np.arange(count)
    earlier = jnp.asarray(order[None, :] < order[:, None])
    rank = ((target[:, None] == target[None, :]) & earlier).astype(i32).sum(1)
    pos = (hot * (2 * start)[None, :]).sum(1) + rank
    place = jnp.arange(2 * pairs_total, dtype=i32)
    entry = jnp.where(place[:, None] == pos[None, :], jnp.asarray(order + 1, i32)[None, :], 0).sum(1)
    pair_ids = jnp.arange(pairs_total, dtype=i32)
    keep = 1 - (pair_ids[:, None] == start[None, :]).any(1).astype(i32)
    end = jnp.maximum(start + pairs - 1, 0)
    return entry, keep, end, cnt


def tables(pattern):
    own_target = jnp.concatenate([pattern[:RIM_ROWS, :K_IN].reshape(-1), pattern[RIM_ROWS:].reshape(-1)])
    rim_rows = np.repeat(np.arange(RIM_ROWS), K - K_IN)
    rim_target = pattern[:RIM_ROWS, K_IN:].reshape(-1) - BLK + jnp.asarray(rim_rows // RIM * RIM, i32)
    entry, keep, end, _ = sorted_lists(own_target, BLK, BLK, np.zeros(BLK), OWN_PAIRS)
    ow = jnp.maximum(entry - 1, 0)
    ob = jnp.where(ow < RIM_ROWS * K_IN, ow // K_IN, RIM_ROWS + (ow - RIM_ROWS * K_IN) // K)
    ou = jnp.where(entry > 0, ob, BLK)
    rbase = np.arange(RIM_ROWS) // RIM * RIM_PAIRS
    rentry, rkeep, rend, rcnt = sorted_lists(rim_target, RIM_ROWS, RIM, rbase, 4 * RIM_PAIRS)
    rw = jnp.maximum(rentry - 1, 0)
    ru = jnp.where(rentry > 0, rw // (K - K_IN), BLK)
    facing = jnp.asarray(np.arange(BLK) // RIM * RIM - BLK, i32)[:, None]
    source = jnp.where(pattern < BLK, pattern, pattern + facing)
    ints = jnp.concatenate([ow, ou, rw, ru, end, rend, source.reshape(-1)]).astype(i32)
    floats = jnp.concatenate([keep, rkeep, (rcnt > 0).astype(i32)]).astype(f32)
    return ints, floats


def kernel(
    tab, ftab, start_ref, w_hbm, out_ref,
    wo, wr, wto, wtr, u, ones, rim, recv_v, recv_t, send_t, recv_d, send_d,
    cur, prev, acc, inv, run_o, run_r, pack, ar1, ar2, ar3,
    w_sem, vs, vr, ts, tr, ds, dr, s1, r1, s2, r2, s3, r3,
):
    ni = lax.axis_index("narrow")
    wi = lax.axis_index("wide")
    n_narrow = lax.axis_size("narrow")
    n_wide = lax.axis_size("wide")
    north = lax.rem(ni + n_narrow - 1, n_narrow)
    south = lax.rem(ni + 1, n_narrow)
    west = lax.rem(wi + n_wide - 1, n_wide)
    east = lax.rem(wi + 1, n_wide)
    neighbours = ({"narrow": north}, {"narrow": south}, {"wide": west}, {"wide": east})
    has = (ni > 0, ni < n_narrow - 1, wi > 0, wi < n_wide - 1)
    wy = wi // Z_CHIPS
    wz = lax.rem(wi, Z_CHIPS)
    group1 = [{"narrow": lax.rem(ni + k, n_narrow)} for k in range(1, 8)]
    group2 = [{"wide": lax.rem(wi + k * Z_CHIPS, n_wide)} for k in range(1, Y_CHIPS)]
    group3 = [{"wide": wy * Z_CHIPS + lax.rem(wz + k, Z_CHIPS)} for k in range(1, Z_CHIPS)]

    barrier = pltpu.get_barrier_semaphore()
    greeted = [{"wide": west}, {"wide": east}] + group1 + group2 + group3
    for peer in greeted:
        pl.semaphore_signal(barrier, inc=1, device_id=peer, device_id_type=MESH)

    rim_copies = []
    for b in range(RIM_ROWS):
        n = K - K_IN
        rim_copies.append(pltpu.make_async_copy(
            w_hbm.at[pl.ds(b * K + K_IN, n)], wr.at[pl.ds(b * n, n)], w_sem.at[b]))
    own_copies = []
    for b in range(BLK):
        n = K_IN if b < RIM_ROWS else K
        own_copies.append(pltpu.make_async_copy(
            w_hbm.at[pl.ds(b * K, n)], wo.at[pl.ds(own_index(b), n)], w_sem.at[RIM_ROWS + b]))
    for copy in rim_copies + own_copies:
        copy.start()

    ones[...] = jnp.ones_like(ones)
    ones[BLK] = jnp.zeros_like(ones[BLK])
    for a in range(3):
        u[a, BLK] = jnp.zeros((NVEC, BS), bf16)

    def pair_product(lhs, w, ow, ou, q):
        left = jnp.concatenate([lhs(tab[ou + 2 * q]), lhs(tab[ou + 2 * q + 1])], axis=1)
        right = jnp.concatenate([w[tab[ow + 2 * q]], w[tab[ow + 2 * q + 1]]], axis=0)
        return jnp.dot(left, right, preferred_element_type=f32)

    def rim_out(lhs, rows, put):
        for d in range(4):
            run = None
            for q in range(d * RIM_PAIRS, (d + 1) * RIM_PAIRS):
                part = pair_product(lhs, wr, O_RW, O_RU, q)
                run = part if run is None else run * ftab[F_RF + q] + part
                run_r[q, 0:rows] = run
            for j in range(RIM):
                e = d * RIM + j
                put(d, j, (run_r[tab[O_RE + e], 0:rows] * ftab[F_NE + e]).astype(bf16))

    def own_back(lhs, rows):
        per = OWN_PAIRS // T_GROUPS

        def body(g, run):
            for q in range(per):
                at = g * per + q
                part = pair_product(lhs, wo, O_OW, O_OU, at)
                run = run * ftab[F_OF + at] + part
                run_o[at, 0:rows] = run
            return run

        lax.fori_loop(0, T_GROUPS, body, jnp.zeros((rows, BS), f32))

    for copy in rim_copies:
        copy.wait()
    for k in range(N_RIM):
        wtr[k] = wr[k].T

    def put_degree(d, j, value):
        send_d[d, j] = value[0:8]

    rim_out(lambda k: ones[k], 16, put_degree)
    pl.semaphore_wait(barrier, len(greeted))
    degree_copies = []
    for d in (2, 3, 0, 1):
        copy = pltpu.make_async_remote_copy(
            send_d.at[d], recv_d.at[OPP[d]], ds.at[d], dr.at[OPP[d]],
            device_id=neighbours[d], device_id_type=MESH)
        copy.start()
        degree_copies.append(copy)

    ones_wide = jnp.ones((16, K * BS), bf16)
    for b in range(BLK):
        n = K_IN if b < RIM_ROWS else K
        o = own_index(b)
        own_copies[b].wait()
        for s in range(n):
            wto[o + s] = wo[o + s].T
        total = jnp.dot(ones_wide[:, : n * BS], wto[o : o + n].reshape(n * BS, BS), preferred_element_type=f32)
        if b < RIM_ROWS:
            m = K - K_IN
            side = jnp.dot(ones_wide[:, : m * BS], wtr[b * m : b * m + m].reshape(m * BS, BS), preferred_element_type=f32)
            total = total + jnp.where(has[b // RIM], side, 0.0)
        inv[b] = total[0:8]
    own_back(lambda k: ones[k], 16)
    for copy in degree_copies:
        copy.wait_recv()
    for b in range(BLK):
        deg = inv[b] + run_o[tab[O_OE + b], 0:8]
        if b < RIM_ROWS:
            deg = deg + jnp.where(has[b // RIM], recv_d[b // RIM, b % RIM].astype(f32), 0.0)
        inv[b] = 1.0 / jnp.sqrt(0.5 * deg)
        x = start_ref[:, b * BS : (b + 1) * BS].astype(f32)
        cur[b] = x
        prev[b] = x
        u[0, b] = (inv[b, 0:1] * x).astype(bf16)
    for copy in degree_copies:
        copy.wait_send()

    def step(a, carry):
        copies = []
        for d in (2, 3, 0, 1):
            copy = pltpu.make_async_remote_copy(
                u.at[a, pl.ds(d * RIM, RIM)], recv_v.at[a, OPP[d]], vs.at[a, d], vr.at[a, OPP[d]],
                device_id=neighbours[d], device_id_type=MESH)
            copy.start()
            copies.append(copy)

        def put_terms(d, j, value):
            send_t[a, d, j] = value

        rim_out(lambda k: u[a, k], NVEC, put_terms)
        term_copies = []
        for d in (2, 3, 0, 1):
            copy = pltpu.make_async_remote_copy(
                send_t.at[a, d], recv_t.at[a, OPP[d]], ts.at[a, d], tr.at[a, OPP[d]],
                device_id=neighbours[d], device_id_type=MESH)
            copy.start()
            term_copies.append(copy)
        own_back(lambda k: u[a, k], NVEC)
        for b in range(BLK):
            n = K_IN if b < RIM_ROWS else K
            o = own_index(b)
            left = jnp.concatenate([u[a, tab[O_PT + b * K + s]] for s in range(n)], axis=1)
            ahead = jnp.dot(left, wto[o : o + n].reshape(n * BS, BS), preferred_element_type=f32)
            acc[b] = ahead + run_o[tab[O_OE + b]]
        for copy in copies:
            copy.wait_recv()
        for d in range(4):
            for j in range(RIM):
                rim[d * RIM + j] = jnp.where(has[d], recv_v[a, d, j], jnp.zeros((NVEC, BS), bf16))
        for b in range(RIM_ROWS):
            m = K - K_IN
            d = b // RIM
            left = jnp.concatenate([rim[tab[O_PT + b * K + K_IN + s]] for s in range(m)], axis=1)
            acc[b] += jnp.dot(left, wtr[b * m : b * m + m].reshape(m * BS, BS), preferred_element_type=f32)
        for copy in term_copies:
            copy.wait_recv()
        alpha = jnp.where(a == 0, 1.0, 2.0).astype(f32) / HALF
        beta = jnp.where(a == 0, 0.0, 1.0).astype(f32)
        nxt = lax.rem(a + 1, 3)
        for b in range(BLK):
            total = acc[b]
            if b < RIM_ROWS:
                total = total + jnp.where(has[b // RIM], recv_t[a, b // RIM, b % RIM].astype(f32), 0.0)
            root = inv[b, 0:1]
            y = cur[b]
            new = alpha * ((y - (0.5 * root) * total) - CENTER * y) - beta * prev[b]
            prev[b] = y
            cur[b] = new
            acc[b] = root * new
        for copy in copies + term_copies:
            copy.wait_send()
        for b in range(BLK):
            u[nxt, b] = acc[b].astype(bf16)
        return carry

    lax.fori_loop(0, 3, step, 0)

    highs = [cur[b].astype(bf16) for b in range(BLK)]
    lows = [(cur[b] - highs[b].astype(f32)).astype(bf16) for b in range(BLK)]
    stacked = jnp.concatenate([jnp.concatenate(highs, axis=1), jnp.concatenate(lows, axis=1)], axis=0)
    product = lax.dot_general(stacked, stacked, (((1,), (1,)), ((), ())), preferred_element_type=f32)
    gram = product[:NVEC, :NVEC] + product[NVEC:, NVEC:] + product[:NVEC, NVEC:] + product[NVEC:, :NVEC]
    packed = jnp.concatenate([gram[8 * g : 8 * g + 8] for g in range(4)], axis=1)

    for group, landing, sends, recvs in ((group1, ar1, s1, r1), (group2, ar2, s2, r2), (group3, ar3, s3, r3)):
        slot = {id(ar1): 0, id(ar2): 1, id(ar3): 2}[id(landing)]
        pack[slot] = packed
        sent = []
        for k, peer in enumerate(group):
            copy = pltpu.make_async_remote_copy(
                pack.at[slot], landing.at[k], sends.at[k], recvs.at[k],
                device_id=peer, device_id_type=MESH)
            copy.start()
            sent.append(copy)
        for copy in sent:
            copy.wait_recv()
        for k in range(len(group)):
            packed = packed + landing[k]
        for copy in sent:
            copy.wait_send()

    lane = lax.broadcasted_iota(i32, (NVEC, BS), 1)
    row = lax.broadcasted_iota(i32, (NVEC, BS), 0)
    moved = jnp.concatenate([pltpu.roll(packed, (96 - 32 * g) % 128, 1) for g in range(4)], axis=0)
    m = jnp.where(lane >= 96, moved, jnp.where(lax.rem(lane, 32) == row, 1.0, 0.0))
    roots = jnp.zeros((NVEC, BS), f32)
    for k in range(NVEC):
        pivot = m[k : k + 1, :]
        d = jnp.broadcast_to(pivot[:, 96 + k : 97 + k], (1, BS))
        column = jnp.broadcast_to(m[:, 96 + k : 97 + k], (NVEC, BS))
        roots = jnp.where(row == k, lax.rsqrt(d), roots)
        m = m - jnp.where(row > k, column, 0.0) * (pivot * (1.0 / d))
    count = n_narrow * n_wide * BLK * BS
    solve = m * roots * math.sqrt(count)
    solve_high = solve.astype(bf16)
    solve_low = (solve - solve_high.astype(f32)).astype(bf16)
    left = jnp.where((lane >= 32) & (lane < 64), solve_low.astype(f32), solve_high.astype(f32))
    left = jnp.where(lane < 96, left, 0.0).astype(bf16)
    for b in range(BLK):
        right = jnp.concatenate([highs[b], highs[b], lows[b], lows[b]], axis=0)
        out_ref[:, b * BS : (b + 1) * BS] = jnp.dot(left, right, preferred_element_type=f32)


def body(start_block, weights, pattern):
    ints, floats = tables(pattern[0, 0])
    dma = pltpu.SemaphoreType.DMA
    vmem = pltpu.VMEM
    out = pl.pallas_call(
        kernel,
        out_shape=jax.ShapeDtypeStruct((NVEC, BLK * BS), f32),
        in_specs=[
            pl.BlockSpec(memory_space=pltpu.SMEM),
            pl.BlockSpec(memory_space=pltpu.SMEM),
            pl.BlockSpec(memory_space=pltpu.VMEM),
            pl.BlockSpec(memory_space=pl.ANY),
        ],
        out_specs=pl.BlockSpec(memory_space=pltpu.VMEM),
        scratch_shapes=[
            vmem((N_OWN, BS, BS), bf16),
            vmem((N_RIM, BS, BS), bf16),
            vmem((N_OWN, BS, BS), bf16),
            vmem((N_RIM, BS, BS), bf16),
            vmem((3, BLK + 1, NVEC, BS), bf16),
            vmem((BLK + 1, 16, BS), bf16),
            vmem((RIM_ROWS, NVEC, BS), bf16),
            vmem((3, 4, RIM, NVEC, BS), bf16),
            vmem((3, 4, RIM, NVEC, BS), bf16),
            vmem((3, 4, RIM, NVEC, BS), bf16),
            vmem((4, RIM, 8, BS), bf16),
            vmem((4, RIM, 8, BS), bf16),
            vmem((BLK, NVEC, BS), f32),
            vmem((BLK, NVEC, BS), f32),
            vmem((BLK, NVEC, BS), f32),
            vmem((BLK, 8, BS), f32),
            vmem((OWN_PAIRS, NVEC, BS), f32),
            vmem((4 * RIM_PAIRS, NVEC, BS), f32),
            vmem((3, 8, BS), f32),
            vmem((7, 8, BS), f32),
            vmem((3, 8, BS), f32),
            vmem((7, 8, BS), f32),
            dma((RIM_ROWS + BLK,)),
            dma((3, 4)),
            dma((3, 4)),
            dma((3, 4)),
            dma((3, 4)),
            dma((4,)),
            dma((4,)),
            dma((7,)),
            dma((7,)),
            dma((3,)),
            dma((3,)),
            dma((7,)),
            dma((7,)),
        ],
        compiler_params=pltpu.CompilerParams(
            collective_id=0, has_side_effects=True, vmem_limit_bytes=56 * 2**20
        ),
        name="filter_step",
    )(ints, floats, start_block[0, 0], weights.reshape(BLK * K, BS, BS))
    return out.reshape(1, 1, NVEC, BLK * BS)


def solution(mesh):
    placed = (
        P("narrow", "wide", None, None),
        P("narrow", "wide", None, None, None, None),
        P("narrow", "wide", None, None),
    )
    return jax.shard_map(
        body, mesh=mesh, in_specs=placed, out_specs=P("narrow", "wide", None, None), check_vma=False
    )
```

```python
import math

import jax
import jax.numpy as jnp
import numpy as np
from jax import lax
from jax.experimental import pallas as pl
from jax.experimental.pallas import tpu as pltpu
from jax.sharding import PartitionSpec as P

f32 = jnp.float32
bf16 = jnp.bfloat16
i32 = jnp.int32
MESH = pl.DeviceIdType.MESH

NVEC = 32
BS = 128
K = 12
K_IN = 9
RIM = 6
BLK = 28
RIM_ROWS = 4 * RIM
LOWER = 0.3
CENTER = (2.0 + LOWER) / 2.0
HALF = (2.0 - LOWER) / 2.0
OPP = (1, 0, 3, 2)

N_OWN = RIM_ROWS * K_IN + (BLK - RIM_ROWS) * K
N_RIM = RIM_ROWS * (K - K_IN)
OWN_PAIRS = (N_OWN + BLK) // 2
RIM_PAIRS = (N_RIM // 4 + RIM) // 2
T_GROUPS = 2
Z_CHIPS = 8
Y_CHIPS = 4

N_POS = 512
OWN_POS = 2 * OWN_PAIRS
CHUNK = 4
SEND_AT = 4
SEGS = BLK + RIM_ROWS


def own_index(b):
    return b * K_IN if b < RIM_ROWS else RIM_ROWS * K_IN + (b - RIM_ROWS) * K


def build_tables(pat_ref, tab_i, tab_f, tab_p, hot_t, padded):
    tab_i[...] = jnp.zeros_like(tab_i)
    tab_f[...] = jnp.zeros_like(tab_f)
    padded[...] = jnp.full((NVEC, BS), 200.0, f32)
    padded[0:BLK, 0:K] = pat_ref[...].astype(f32)
    lane = lax.broadcasted_iota(i32, (NVEC, BS), 1)
    row = lax.broadcasted_iota(i32, (NVEC, BS), 0)
    face = jnp.where(row >= RIM, 1.0, 0.0) + jnp.where(row >= 2 * RIM, 1.0, 0.0) + jnp.where(row >= 3 * RIM, 1.0, 0.0)
    t = padded[...]
    t = jnp.where((t >= BLK) & (t < 100), t + RIM * face, t)
    tab_p[...] = jnp.clip(jnp.where(t < BLK, t, t - BLK), 0.0, BLK - 1.0).astype(i32)
    rows = K * NVEC
    column = jnp.concatenate([jnp.broadcast_to(t[:, s : s + 1], (NVEC, BS)) for s in range(K)], axis=0)
    seg = lax.broadcasted_iota(i32, (rows, BS), 1).astype(f32)
    hot = jnp.where(column == seg, 1.0, 0.0)
    hot_t[...] = hot.T[0 : hot_t.shape[0]].astype(bf16)
    hot_b = hot.astype(bf16)
    lower = lax.broadcasted_iota(i32, (rows, rows), 0) > lax.broadcasted_iota(i32, (rows, rows), 1)
    before = jnp.dot(jnp.where(lower, 1.0, 0.0).astype(bf16), hot_b, preferred_element_type=f32)
    ones8 = jnp.ones((8, rows), bf16)
    count = jnp.dot(ones8, hot_b, preferred_element_type=f32)
    pairs = jnp.floor((count + 1.0) * 0.5)

    def group(e):
        total = jnp.zeros(e.shape, f32)
        for r in range(4):
            total = total + jnp.where(e >= BLK + r * RIM, 1.0, 0.0)
        return total

    e0 = lax.broadcasted_iota(i32, (BS, BS), 0)
    e1 = lax.broadcasted_iota(i32, (BS, BS), 1)
    earlier = jnp.where((e0 < e1) & (group(e0) == group(e1)), 1.0, 0.0).astype(bf16)
    e8 = lax.broadcasted_iota(i32, (8, BS), 1)
    g8 = group(e8)
    base = jnp.where(g8 > 0, OWN_PAIRS + (g8 - 1.0) * RIM_PAIRS, 0.0)
    start = jnp.dot(pairs.astype(bf16), earlier, preferred_element_type=f32) + base
    rank = jnp.sum(hot * before, axis=1, keepdims=True)
    first = jnp.sum(hot * (2.0 * start[0:1]), axis=1, keepdims=True)
    valid = column[:, 0:1] < 100.0
    pos = jnp.where(valid, rank + first, -1.0)
    place = lax.broadcasted_iota(i32, (rows, N_POS), 1).astype(f32)
    at = jnp.where(pos == place, 1.0, 0.0)
    entry = lax.broadcasted_iota(i32, (8, rows), 1)
    which = lax.broadcasted_iota(i32, (8, rows), 0)
    vals = jnp.where(which == 0, (entry & 31) + 1, jnp.where(which == 1, entry >> 5, 0)).astype(f32).astype(bf16)
    found = jnp.dot(vals, at.astype(bf16), preferred_element_type=f32)
    opens = jnp.dot(ones8, jnp.where(rank == 0.0, at, 0.0).astype(bf16), preferred_element_type=f32)
    b = found[0:1] - 1.0
    s = found[1:2]
    p = lax.broadcasted_iota(i32, (1, N_POS), 1)
    own_w = jnp.where(b < RIM_ROWS, b * K_IN + s, RIM_ROWS * K_IN + (b - RIM_ROWS) * K + s)
    rim_w = jnp.clip(b * (K - K_IN) + s - K_IN, 0.0, N_RIM - 1.0)
    w = jnp.where(p < OWN_POS, jnp.clip(own_w, 0.0, N_OWN - 1.0), rim_w)
    source = jnp.where(b >= 0, jnp.minimum(b, BLK - 1.0), float(BLK))
    end = start + pairs - 1.0
    end = jnp.where(g8 > 0, jnp.clip(end - OWN_PAIRS, 0.0, 4 * RIM_PAIRS - 1.0), jnp.clip(end, 0.0, OWN_PAIRS - 1.0))
    tab_i[0:1, :] = w.astype(i32)
    tab_i[1:2, :] = source.astype(i32)
    tab_i[2:3, 0:BS] = end[0:1].astype(i32)
    tab_f[0:1, :] = 1.0 - opens[0:1]
    tab_f[1:2, 0:BS] = jnp.where(count[0:1] > 0, 1.0, 0.0)


def kernel(
    tab, ftab, ptab, hot_t, start_ref, w_hbm, out_ref,
    wo, wr, wto, wtr, u, rim, recv_v, recv_t, send_t, recv_d, send_d,
    cur, prev, acc, inv, run_o, run_r, pack, ar1, ar2, ar3,
    sums, rowsum,
    w_sem, vs, vr, ts, tr, ds, dr, s1, r1, s2, r2, s3, r3,
):
    ni = lax.axis_index("narrow")
    wi = lax.axis_index("wide")
    n_narrow = lax.axis_size("narrow")
    n_wide = lax.axis_size("wide")
    north = lax.rem(ni + n_narrow - 1, n_narrow)
    south = lax.rem(ni + 1, n_narrow)
    west = lax.rem(wi + n_wide - 1, n_wide)
    east = lax.rem(wi + 1, n_wide)
    neighbours = ({"narrow": north}, {"narrow": south}, {"wide": west}, {"wide": east})
    has = (ni > 0, ni < n_narrow - 1, wi > 0, wi < n_wide - 1)
    wy = wi // Z_CHIPS
    wz = lax.rem(wi, Z_CHIPS)
    group1 = [{"narrow": lax.rem(ni + k, n_narrow)} for k in range(1, 8)]
    group2 = [{"wide": lax.rem(wi + k * Z_CHIPS, n_wide)} for k in range(1, Y_CHIPS)]
    group3 = [{"wide": wy * Z_CHIPS + lax.rem(wz + k, Z_CHIPS)} for k in range(1, Z_CHIPS)]

    barrier = pltpu.get_barrier_semaphore()
    greeted = [{"wide": west}, {"wide": east}] + group1 + group2 + group3
    for peer in greeted:
        pl.semaphore_signal(barrier, inc=1, device_id=peer, device_id_type=MESH)

    rim_copies = []
    for b in range(RIM_ROWS):
        n = K - K_IN
        rim_copies.append(pltpu.make_async_copy(
            w_hbm.at[pl.ds(b * K + K_IN, n)], wr.at[pl.ds(b * n, n)], w_sem.at[b]))
    own_copies = []
    for b in range(BLK):
        n = K_IN if b < RIM_ROWS else K
        own_copies.append(pltpu.make_async_copy(
            w_hbm.at[pl.ds(b * K, n)], wo.at[pl.ds(own_index(b), n)], w_sem.at[RIM_ROWS + b]))
    for copy in rim_copies + own_copies:
        copy.start()

    for a in range(3):
        u[a, BLK] = jnp.zeros((NVEC, BS), bf16)
    sums[...] = jnp.zeros_like(sums)

    def pair_product(lhs, w, at):
        left = jnp.concatenate([lhs(tab[1, at]), lhs(tab[1, at + 1])], axis=1)
        right = jnp.concatenate([w[tab[0, at]], w[tab[0, at + 1]]], axis=0)
        return jnp.dot(left, right, preferred_element_type=f32)

    def rim_out(lhs, d, put):
        run = None
        for q in range(d * RIM_PAIRS, (d + 1) * RIM_PAIRS):
            at = OWN_POS + 2 * q
            part = pair_product(lhs, wr, at)
            run = part if run is None else run * ftab[0, at] + part
            run_r[q] = run
        for j in range(RIM):
            e = BLK + d * RIM + j
            put(d, j, (run_r[tab[2, e]] * ftab[1, e]).astype(bf16))

    def own_back(lhs):
        per = OWN_PAIRS // T_GROUPS

        def body(g, run):
            for q in range(per):
                at = g * per + q
                part = pair_product(lhs, wo, 2 * at)
                run = run * ftab[0, 2 * at] + part
                run_o[at] = run
            return run

        lax.fori_loop(0, T_GROUPS, body, jnp.zeros((NVEC, BS), f32))

    ones8 = jnp.ones((8, K * BS), bf16)

    def column_sums(w, first, n, b, s0):
        wide = jnp.concatenate([w[first + s] for s in range(n)], axis=1)
        total = jnp.dot(ones8[:, :BS], wide, preferred_element_type=f32)
        for s in range(n):
            at = (s0 + s) * NVEC + b
            sums[at : at + 1] = total[0:1, s * BS : (s + 1) * BS]

    def row_sums(wt, first, n):
        return jnp.dot(ones8[:, : n * BS], wt[first : first + n].reshape(n * BS, BS), preferred_element_type=f32)

    def grouped_sums():
        high = sums[...].astype(bf16)
        low = (sums[...] - high.astype(f32)).astype(bf16)
        return jnp.dot(hot_t[...], high, preferred_element_type=f32) + jnp.dot(
            hot_t[...], low, preferred_element_type=f32)

    for copy in rim_copies:
        copy.wait()
    m = K - K_IN
    for b in range(RIM_ROWS):
        for s in range(m):
            wtr[b * m + s] = wr[b * m + s].T
        column_sums(wr, b * m, m, b, K_IN)
    degree_copies = []

    def send_degree():
        out = grouped_sums()
        for d in range(4):
            at = BLK + d * RIM
            send_d[d, 0:RIM] = out[at : at + RIM].astype(bf16)
        pl.semaphore_wait(barrier, len(greeted))
        for d in (2, 3, 0, 1):
            copy = pltpu.make_async_remote_copy(
                send_d.at[d], recv_d.at[OPP[d]], ds.at[d], dr.at[OPP[d]],
                device_id=neighbours[d], device_id_type=MESH)
            copy.start()
            degree_copies.append(copy)

    def own_row_sums(b):
        total = row_sums(wto, own_index(b), K_IN if b < RIM_ROWS else K)
        if b < RIM_ROWS:
            total = total + jnp.where(has[b // RIM], row_sums(wtr, b * m, m), 0.0)
        rowsum[b : b + 1] = total[0:1]

    rowsum[...] = jnp.ones_like(rowsum)
    send_d[...] = jnp.zeros_like(send_d)
    chunks = [range(c, c + CHUNK) for c in range(0, BLK, CHUNK)]
    for c, chunk in enumerate(chunks):
        for b in chunk:
            own_copies[b].wait()
        if c == SEND_AT:
            send_degree()
        for b in chunk:
            n = K_IN if b < RIM_ROWS else K
            for s in range(n):
                wto[own_index(b) + s] = wo[own_index(b) + s].T
            column_sums(wo, own_index(b), n, b, 0)
        if c > 0:
            for b in chunks[c - 1]:
                own_row_sums(b)
    for b in chunks[-1]:
        own_row_sums(b)
    back = grouped_sums()
    degree = rowsum[...] + back[0:NVEC]
    rowsum[...] = degree
    for copy in degree_copies:
        copy.wait_recv()
    for d in range(4):
        at = d * RIM
        arrived = jnp.where(has[d], recv_d[d].astype(f32), 0.0)
        rowsum[at : at + RIM] = rowsum[at : at + RIM] + arrived[0:RIM]
    inv[...] = 1.0 / jnp.sqrt(0.5 * rowsum[...])
    for b in range(BLK):
        x = start_ref[:, b * BS : (b + 1) * BS].astype(f32)
        cur[b] = x
        prev[b] = x
        u[0, b] = (inv[b : b + 1] * x).astype(bf16)
    for copy in degree_copies:
        copy.wait_send()
    def step(a, carry):
        copies = []
        for d in (2, 3, 0, 1):
            copy = pltpu.make_async_remote_copy(
                u.at[a, pl.ds(d * RIM, RIM)], recv_v.at[a, OPP[d]], vs.at[a, d], vr.at[a, OPP[d]],
                device_id=neighbours[d], device_id_type=MESH)
            copy.start()
            copies.append(copy)

        def put_terms(d, j, value):
            send_t[a, d, j] = value

        term_copies = []
        for pair in ((2, 3), (0, 1)):
            for d in pair:
                rim_out(lambda k: u[a, k], d, put_terms)
            for d in pair:
                copy = pltpu.make_async_remote_copy(
                    send_t.at[a, d], recv_t.at[a, OPP[d]], ts.at[a, d], tr.at[a, OPP[d]],
                    device_id=neighbours[d], device_id_type=MESH)
                copy.start()
                term_copies.append(copy)
        own_back(lambda k: u[a, k])
        for b in range(BLK):
            n = K_IN if b < RIM_ROWS else K
            o = own_index(b)
            left = jnp.concatenate([u[a, ptab[b, s]] for s in range(n)], axis=1)
            ahead = jnp.dot(left, wto[o : o + n].reshape(n * BS, BS), preferred_element_type=f32)
            acc[b] = ahead + run_o[tab[2, b]]
        for copy in copies:
            copy.wait_recv()
        for d in range(4):
            for j in range(RIM):
                rim[d * RIM + j] = jnp.where(has[d], recv_v[a, d, j], jnp.zeros((NVEC, BS), bf16))
        for b in range(RIM_ROWS):
            left = jnp.concatenate([rim[jnp.minimum(ptab[b, K_IN + s], RIM_ROWS - 1)] for s in range(m)], axis=1)
            acc[b] += jnp.dot(left, wtr[b * m : b * m + m].reshape(m * BS, BS), preferred_element_type=f32)
        for copy in term_copies:
            copy.wait_recv()
        alpha = jnp.where(a == 0, 1.0, 2.0).astype(f32) / HALF
        beta = jnp.where(a == 0, 0.0, 1.0).astype(f32)
        nxt = lax.rem(a + 1, 3)
        for b in range(BLK):
            total = acc[b]
            if b < RIM_ROWS:
                total = total + jnp.where(has[b // RIM], recv_t[a, b // RIM, b % RIM].astype(f32), 0.0)
            root = inv[b : b + 1]
            y = cur[b]
            new = alpha * ((y - (0.5 * root) * total) - CENTER * y) - beta * prev[b]
            prev[b] = y
            cur[b] = new
            acc[b] = root * new
        for copy in copies + term_copies:
            copy.wait_send()
        for b in range(BLK):
            u[nxt, b] = acc[b].astype(bf16)
        return carry

    lax.fori_loop(0, 3, step, 0)

    highs = [cur[b].astype(bf16) for b in range(BLK)]
    lows = [(cur[b] - highs[b].astype(f32)).astype(bf16) for b in range(BLK)]
    stacked = jnp.concatenate([jnp.concatenate(highs, axis=1), jnp.concatenate(lows, axis=1)], axis=0)
    product = lax.dot_general(stacked, stacked, (((1,), (1,)), ((), ())), preferred_element_type=f32)
    gram = product[:NVEC, :NVEC] + product[NVEC:, NVEC:] + product[:NVEC, NVEC:] + product[NVEC:, :NVEC]
    packed = jnp.concatenate([gram[8 * g : 8 * g + 8] for g in range(4)], axis=1)

    for group, landing, sends, recvs in ((group1, ar1, s1, r1), (group2, ar2, s2, r2), (group3, ar3, s3, r3)):
        slot = {id(ar1): 0, id(ar2): 1, id(ar3): 2}[id(landing)]
        pack[slot] = packed
        sent = []
        for k, peer in enumerate(group):
            copy = pltpu.make_async_remote_copy(
                pack.at[slot], landing.at[k], sends.at[k], recvs.at[k],
                device_id=peer, device_id_type=MESH)
            copy.start()
            sent.append(copy)
        for copy in sent:
            copy.wait_recv()
        for k in range(len(group)):
            packed = packed + landing[k]
        for copy in sent:
            copy.wait_send()

    lane = lax.broadcasted_iota(i32, (NVEC, BS), 1)
    row = lax.broadcasted_iota(i32, (NVEC, BS), 0)
    moved = jnp.concatenate([pltpu.roll(packed, (96 - 32 * g) % 128, 1) for g in range(4)], axis=0)
    m = jnp.where(lane >= 96, moved, jnp.where(lax.rem(lane, 32) == row, 1.0, 0.0))
    roots = jnp.zeros((NVEC, BS), f32)
    for k in range(NVEC):
        pivot = m[k : k + 1, :]
        d = jnp.broadcast_to(pivot[:, 96 + k : 97 + k], (1, BS))
        column = jnp.broadcast_to(m[:, 96 + k : 97 + k], (NVEC, BS))
        roots = jnp.where(row == k, lax.rsqrt(d), roots)
        m = m - jnp.where(row > k, column, 0.0) * (pivot * (1.0 / d))
    count = n_narrow * n_wide * BLK * BS
    solve = m * roots * math.sqrt(count)
    solve_high = solve.astype(bf16)
    solve_low = (solve - solve_high.astype(f32)).astype(bf16)
    left = jnp.where((lane >= 32) & (lane < 64), solve_low.astype(f32), solve_high.astype(f32))
    left = jnp.where(lane < 96, left, 0.0).astype(bf16)
    for b in range(BLK):
        right = jnp.concatenate([highs[b], highs[b], lows[b], lows[b]], axis=0)
        out_ref[:, b * BS : (b + 1) * BS] = jnp.dot(left, right, preferred_element_type=f32)


def tables(pattern):
    return pl.pallas_call(
        build_tables,
        out_shape=[
            jax.ShapeDtypeStruct((8, N_POS), i32),
            jax.ShapeDtypeStruct((8, N_POS), f32),
            jax.ShapeDtypeStruct((NVEC, BS), i32),
            jax.ShapeDtypeStruct((64, K * NVEC), bf16),
        ],
        in_specs=[pl.BlockSpec(memory_space=pltpu.VMEM)],
        out_specs=[pl.BlockSpec(memory_space=pltpu.VMEM)] * 4,
        scratch_shapes=[pltpu.VMEM((NVEC, BS), f32)],
        compiler_params=pltpu.CompilerParams(vmem_limit_bytes=16 * 2**20),
        name="index_tables",
    )(pattern)


def body(start_block, weights, pattern):
    dma = pltpu.SemaphoreType.DMA
    vmem = pltpu.VMEM
    out = pl.pallas_call(
        kernel,
        out_shape=jax.ShapeDtypeStruct((NVEC, BLK * BS), f32),
        in_specs=[
            pl.BlockSpec(memory_space=pltpu.SMEM),
            pl.BlockSpec(memory_space=pltpu.SMEM),
            pl.BlockSpec(memory_space=pltpu.SMEM),
            pl.BlockSpec(memory_space=pltpu.VMEM),
            pl.BlockSpec(memory_space=pltpu.VMEM),
            pl.BlockSpec(memory_space=pl.ANY),
        ],
        out_specs=pl.BlockSpec(memory_space=pltpu.VMEM),
        scratch_shapes=[
            vmem((N_OWN, BS, BS), bf16),
            vmem((N_RIM, BS, BS), bf16),
            vmem((N_OWN, BS, BS), bf16),
            vmem((N_RIM, BS, BS), bf16),
            vmem((3, BLK + 1, NVEC, BS), bf16),
            vmem((RIM_ROWS, NVEC, BS), bf16),
            vmem((3, 4, RIM, NVEC, BS), bf16),
            vmem((3, 4, RIM, NVEC, BS), bf16),
            vmem((3, 4, RIM, NVEC, BS), bf16),
            vmem((4, 8, BS), bf16),
            vmem((4, 8, BS), bf16),
            vmem((BLK, NVEC, BS), f32),
            vmem((BLK, NVEC, BS), f32),
            vmem((BLK, NVEC, BS), f32),
            vmem((NVEC, BS), f32),
            vmem((OWN_PAIRS, NVEC, BS), f32),
            vmem((4 * RIM_PAIRS, NVEC, BS), f32),
            vmem((3, 8, BS), f32),
            vmem((7, 8, BS), f32),
            vmem((3, 8, BS), f32),
            vmem((7, 8, BS), f32),
            vmem((K * NVEC, BS), f32),
            vmem((NVEC, BS), f32),
            dma((RIM_ROWS + BLK,)),
            dma((3, 4)),
            dma((3, 4)),
            dma((3, 4)),
            dma((3, 4)),
            dma((4,)),
            dma((4,)),
            dma((7,)),
            dma((7,)),
            dma((3,)),
            dma((3,)),
            dma((7,)),
            dma((7,)),
        ],
        compiler_params=pltpu.CompilerParams(
            collective_id=0, has_side_effects=True, vmem_limit_bytes=56 * 2**20
        ),
        name="filter_step",
    )(*tables(pattern[0, 0]), start_block[0, 0], weights.reshape(BLK * K, BS, BS))
    return out.reshape(1, 1, NVEC, BLK * BS)


def solution(mesh):
    placed = (
        P("narrow", "wide", None, None),
        P("narrow", "wide", None, None, None, None),
        P("narrow", "wide", None, None),
    )
    return jax.shard_map(
        body, mesh=mesh, in_specs=placed, out_specs=P("narrow", "wide", None, None), check_vma=False
    )
```

```python
import math

import jax
import jax.numpy as jnp
import numpy as np
from jax import lax
from jax.experimental import pallas as pl
from jax.experimental.pallas import tpu as pltpu
from jax.sharding import PartitionSpec as P

f32 = jnp.float32
bf16 = jnp.bfloat16
i32 = jnp.int32
MESH = pl.DeviceIdType.MESH

NVEC = 32
BS = 128
K = 12
K_IN = 9
RIM = 6
BLK = 28
RIM_ROWS = 4 * RIM
LOWER = 0.3
CENTER = (2.0 + LOWER) / 2.0
HALF = (2.0 - LOWER) / 2.0
OPP = (1, 0, 3, 2)

N_OWN = RIM_ROWS * K_IN + (BLK - RIM_ROWS) * K
N_RIM = RIM_ROWS * (K - K_IN)
OWN_PAIRS = (N_OWN + BLK) // 2
RIM_PAIRS = (N_RIM // 4 + RIM) // 2
T_GROUPS = 2
Z_CHIPS = 8
Y_CHIPS = 4

N_POS = 512
OWN_POS = 2 * OWN_PAIRS
CHUNK = 4
SEND_AT = 4
SEGS = BLK + RIM_ROWS


def own_index(b):
    return b * K_IN if b < RIM_ROWS else RIM_ROWS * K_IN + (b - RIM_ROWS) * K


def build_tables(pat_ref, tab_i, tab_f, tab_p, hot_t, padded):
    tab_i[...] = jnp.zeros_like(tab_i)
    tab_f[...] = jnp.zeros_like(tab_f)
    padded[...] = jnp.full((NVEC, BS), 200.0, f32)
    for k in range(K):
        padded[k : k + 1, 0:BLK] = pat_ref[k].astype(f32)
    turned = padded[...].T[0:NVEC]
    padded[...] = jnp.full((NVEC, BS), 200.0, f32)
    padded[:, 0:NVEC] = turned
    lane = lax.broadcasted_iota(i32, (NVEC, BS), 1)
    row = lax.broadcasted_iota(i32, (NVEC, BS), 0)
    face = jnp.where(row >= RIM, 1.0, 0.0) + jnp.where(row >= 2 * RIM, 1.0, 0.0) + jnp.where(row >= 3 * RIM, 1.0, 0.0)
    t = padded[...]
    t = jnp.where((t >= BLK) & (t < 100), t + RIM * face, t)
    tab_p[...] = jnp.clip(jnp.where(t < BLK, t, t - BLK), 0.0, BLK - 1.0).astype(i32)
    rows = K * NVEC
    column = jnp.concatenate([jnp.broadcast_to(t[:, s : s + 1], (NVEC, BS)) for s in range(K)], axis=0)
    seg = lax.broadcasted_iota(i32, (rows, BS), 1).astype(f32)
    hot = jnp.where(column == seg, 1.0, 0.0)
    hot_t[...] = hot.T[0 : hot_t.shape[0]].astype(bf16)
    hot_b = hot.astype(bf16)
    lower = lax.broadcasted_iota(i32, (rows, rows), 0) > lax.broadcasted_iota(i32, (rows, rows), 1)
    before = jnp.dot(jnp.where(lower, 1.0, 0.0).astype(bf16), hot_b, preferred_element_type=f32)
    ones8 = jnp.ones((8, rows), bf16)
    count = jnp.dot(ones8, hot_b, preferred_element_type=f32)
    pairs = jnp.floor((count + 1.0) * 0.5)

    def group(e):
        total = jnp.zeros(e.shape, f32)
        for r in range(4):
            total = total + jnp.where(e >= BLK + r * RIM, 1.0, 0.0)
        return total

    e0 = lax.broadcasted_iota(i32, (BS, BS), 0)
    e1 = lax.broadcasted_iota(i32, (BS, BS), 1)
    earlier = jnp.where((e0 < e1) & (group(e0) == group(e1)), 1.0, 0.0).astype(bf16)
    e8 = lax.broadcasted_iota(i32, (8, BS), 1)
    g8 = group(e8)
    base = jnp.where(g8 > 0, OWN_PAIRS + (g8 - 1.0) * RIM_PAIRS, 0.0)
    start = jnp.dot(pairs.astype(bf16), earlier, preferred_element_type=f32) + base
    rank = jnp.sum(hot * before, axis=1, keepdims=True)
    first = jnp.sum(hot * (2.0 * start[0:1]), axis=1, keepdims=True)
    valid = column[:, 0:1] < 100.0
    pos = jnp.where(valid, rank + first, -1.0)
    place = lax.broadcasted_iota(i32, (rows, N_POS), 1).astype(f32)
    at = jnp.where(pos == place, 1.0, 0.0)
    entry = lax.broadcasted_iota(i32, (8, rows), 1)
    which = lax.broadcasted_iota(i32, (8, rows), 0)
    vals = jnp.where(which == 0, (entry & 31) + 1, jnp.where(which == 1, entry >> 5, 0)).astype(f32).astype(bf16)
    found = jnp.dot(vals, at.astype(bf16), preferred_element_type=f32)
    opens = jnp.dot(ones8, jnp.where(rank == 0.0, at, 0.0).astype(bf16), preferred_element_type=f32)
    b = found[0:1] - 1.0
    s = found[1:2]
    p = lax.broadcasted_iota(i32, (1, N_POS), 1)
    own_w = jnp.where(b < RIM_ROWS, b * K_IN + s, RIM_ROWS * K_IN + (b - RIM_ROWS) * K + s)
    rim_w = jnp.clip(b * (K - K_IN) + s - K_IN, 0.0, N_RIM - 1.0)
    w = jnp.where(p < OWN_POS, jnp.clip(own_w, 0.0, N_OWN - 1.0), rim_w)
    source = jnp.where(b >= 0, jnp.minimum(b, BLK - 1.0), float(BLK))
    end = start + pairs - 1.0
    end = jnp.where(g8 > 0, jnp.clip(end - OWN_PAIRS, 0.0, 4 * RIM_PAIRS - 1.0), jnp.clip(end, 0.0, OWN_PAIRS - 1.0))
    tab_i[0:1, :] = w.astype(i32)
    tab_i[1:2, :] = source.astype(i32)
    tab_i[2:3, 0:BS] = end[0:1].astype(i32)
    tab_f[0:1, :] = 1.0 - opens[0:1]
    tab_f[1:2, 0:BS] = jnp.where(count[0:1] > 0, 1.0, 0.0)


def kernel(
    tab, ftab, ptab, hot_t, start_ref, w_hbm, solve_ref, cur,
    wo, wr, wto, wtr, u, rim, recv_v, recv_t, send_t, recv_d, send_d,
    prev, acc, inv, run_o, run_r, pack, ar1, ar2, ar3,
    sums, rowsum, recv_x, send_i, recv_i,
    w_sem, xs, xr, rs, rr, vs, vr, ts, tr, ds, dr, s1, r1, s2, r2, s3, r3,
):
    ni = lax.axis_index("narrow")
    wi = lax.axis_index("wide")
    n_narrow = lax.axis_size("narrow")
    n_wide = lax.axis_size("wide")
    north = lax.rem(ni + n_narrow - 1, n_narrow)
    south = lax.rem(ni + 1, n_narrow)
    west = lax.rem(wi + n_wide - 1, n_wide)
    east = lax.rem(wi + 1, n_wide)
    neighbours = ({"narrow": north}, {"narrow": south}, {"wide": west}, {"wide": east})
    has = (ni > 0, ni < n_narrow - 1, wi > 0, wi < n_wide - 1)
    wy = wi // Z_CHIPS
    wz = lax.rem(wi, Z_CHIPS)
    group1 = [{"narrow": lax.rem(ni + k, n_narrow)} for k in range(1, 8)]
    group2 = [{"wide": lax.rem(wi + k * Z_CHIPS, n_wide)} for k in range(1, Y_CHIPS)]
    group3 = [{"wide": wy * Z_CHIPS + lax.rem(wz + k, Z_CHIPS)} for k in range(1, Z_CHIPS)]

    barrier = pltpu.get_barrier_semaphore()
    greeted = [{"wide": west}, {"wide": east}] + group1 + group2 + group3
    for peer in greeted:
        pl.semaphore_signal(barrier, inc=1, device_id=peer, device_id_type=MESH)

    rim_copies = []
    for b in range(RIM_ROWS):
        n = K - K_IN
        rim_copies.append(pltpu.make_async_copy(
            w_hbm.at[pl.ds(b * K + K_IN, n)], wr.at[pl.ds(b * n, n)], w_sem.at[b]))
    own_copies = []
    for b in range(BLK):
        n = K_IN if b < RIM_ROWS else K
        own_copies.append(pltpu.make_async_copy(
            w_hbm.at[pl.ds(b * K, n)], wo.at[pl.ds(own_index(b), n)], w_sem.at[RIM_ROWS + b]))
    for copy in rim_copies + own_copies:
        copy.start()

    for a in range(3):
        u[a, BLK] = jnp.zeros((NVEC, BS), bf16)
    sums[...] = jnp.zeros_like(sums)

    def pair_product(lhs, w, at):
        left = jnp.concatenate([lhs(tab[1, at]), lhs(tab[1, at + 1])], axis=1)
        right = jnp.concatenate([w[tab[0, at]], w[tab[0, at + 1]]], axis=0)
        return jnp.dot(left, right, preferred_element_type=f32)

    def rim_out(lhs, d, put):
        run = None
        for q in range(d * RIM_PAIRS, (d + 1) * RIM_PAIRS):
            at = OWN_POS + 2 * q
            part = pair_product(lhs, wr, at)
            run = part if run is None else run * ftab[0, at] + part
            run_r[q] = run
        for j in range(RIM):
            e = BLK + d * RIM + j
            put(d, j, (run_r[tab[2, e]] * ftab[1, e]).astype(bf16))

    def own_back(lhs):
        per = OWN_PAIRS // T_GROUPS

        def body(g, run):
            for q in range(per):
                at = g * per + q
                part = pair_product(lhs, wo, 2 * at)
                run = run * ftab[0, 2 * at] + part
                run_o[at] = run
            return run

        lax.fori_loop(0, T_GROUPS, body, jnp.zeros((NVEC, BS), f32))

    ones8 = jnp.ones((8, K * BS), bf16)

    def column_sums(w, first, n, b, s0):
        wide = jnp.concatenate([w[first + s] for s in range(n)], axis=1)
        total = jnp.dot(ones8[:, :BS], wide, preferred_element_type=f32)
        for s in range(n):
            at = (s0 + s) * NVEC + b
            sums[at : at + 1] = total[0:1, s * BS : (s + 1) * BS]

    def row_sums(wt, first, n):
        return jnp.dot(ones8[:, : n * BS], wt[first : first + n].reshape(n * BS, BS), preferred_element_type=f32)

    def grouped_sums():
        high = sums[...].astype(bf16)
        low = (sums[...] - high.astype(f32)).astype(bf16)
        return jnp.dot(hot_t[...], high, preferred_element_type=f32) + jnp.dot(
            hot_t[...], low, preferred_element_type=f32)

    for copy in rim_copies:
        copy.wait()
    m = K - K_IN
    for b in range(RIM_ROWS):
        for s in range(m):
            wtr[b * m + s] = wr[b * m + s].T
        column_sums(wr, b * m, m, b, K_IN)
    degree_copies = []
    start_copies = []

    def send_degree():
        out = grouped_sums()
        for d in range(4):
            at = BLK + d * RIM
            send_d[d, 0:RIM] = out[at : at + RIM].astype(bf16)
        pl.semaphore_wait(barrier, len(greeted))
        for d in (2, 3, 0, 1):
            copy = pltpu.make_async_remote_copy(
                send_d.at[d], recv_d.at[OPP[d]], ds.at[d], dr.at[OPP[d]],
                device_id=neighbours[d], device_id_type=MESH)
            copy.start()
            degree_copies.append(copy)
        for d in (2, 3, 0, 1):
            copy = pltpu.make_async_remote_copy(
                start_ref.at[:, pl.ds(d * RIM * BS, RIM * BS)], recv_x.at[OPP[d]], xs.at[d], xr.at[OPP[d]],
                device_id=neighbours[d], device_id_type=MESH)
            copy.start()
            start_copies.append(copy)

    def own_row_sums(b):
        total = row_sums(wto, own_index(b), K_IN if b < RIM_ROWS else K)
        if b < RIM_ROWS:
            total = total + jnp.where(has[b // RIM], row_sums(wtr, b * m, m), 0.0)
        rowsum[b : b + 1] = total[0:1]

    rowsum[...] = jnp.ones_like(rowsum)
    send_d[...] = jnp.zeros_like(send_d)
    send_i[...] = jnp.zeros_like(send_i)
    chunks = [range(c, c + CHUNK) for c in range(0, BLK, CHUNK)]
    for c, chunk in enumerate(chunks):
        for b in chunk:
            own_copies[b].wait()
        if c == SEND_AT:
            send_degree()
        for b in chunk:
            n = K_IN if b < RIM_ROWS else K
            for s in range(n):
                wto[own_index(b) + s] = wo[own_index(b) + s].T
            column_sums(wo, own_index(b), n, b, 0)
        if c > 0:
            for b in chunks[c - 1]:
                own_row_sums(b)
    for b in chunks[-1]:
        own_row_sums(b)
    back = grouped_sums()
    degree = rowsum[...] + back[0:NVEC]
    rowsum[...] = degree
    for copy in degree_copies:
        copy.wait_recv()
    for d in range(4):
        at = d * RIM
        arrived = jnp.where(has[d], recv_d[d].astype(f32), 0.0)
        rowsum[at : at + RIM] = rowsum[at : at + RIM] + arrived[0:RIM]
    inv[...] = 1.0 / jnp.sqrt(0.5 * rowsum[...])
    root_copies = []
    for d in (2, 3, 0, 1):
        send_i[d, 0:RIM] = inv[d * RIM : d * RIM + RIM]
    for d in (2, 3, 0, 1):
        copy = pltpu.make_async_remote_copy(
            send_i.at[d], recv_i.at[OPP[d]], rs.at[d], rr.at[OPP[d]],
            device_id=neighbours[d], device_id_type=MESH)
        copy.start()
        root_copies.append(copy)
    for b in range(BLK):
        x = start_ref[:, b * BS : (b + 1) * BS].astype(f32)
        cur[b] = x
        prev[b] = x
        u[0, b] = (inv[b : b + 1] * x).astype(bf16)
    for copy in degree_copies:
        copy.wait_send()
    def step(a, carry):
        copies = []
        for d in (2, 3, 0, 1):
            copies.append(pltpu.make_async_remote_copy(
                u.at[a, pl.ds(d * RIM, RIM)], recv_v.at[a, OPP[d]], vs.at[a, d], vr.at[a, OPP[d]],
                device_id=neighbours[d], device_id_type=MESH))

        @pl.when(a > 0)
        def _():
            for copy in copies:
                copy.start()

        def put_terms(d, j, value):
            send_t[a, d, j] = value

        term_copies = []
        for pair in ((2, 3), (0, 1)):
            for d in pair:
                rim_out(lambda k: u[a, k], d, put_terms)
            for d in pair:
                copy = pltpu.make_async_remote_copy(
                    send_t.at[a, d], recv_t.at[a, OPP[d]], ts.at[a, d], tr.at[a, OPP[d]],
                    device_id=neighbours[d], device_id_type=MESH)
                copy.start()
                term_copies.append(copy)
        own_back(lambda k: u[a, k])
        for b in range(BLK):
            n = K_IN if b < RIM_ROWS else K
            o = own_index(b)
            left = jnp.concatenate([u[a, ptab[b, s]] for s in range(n)], axis=1)
            ahead = jnp.dot(left, wto[o : o + n].reshape(n * BS, BS), preferred_element_type=f32)
            acc[b] = ahead + run_o[tab[2, b]]
        @pl.when(a == 0)
        def _():
            for copy in start_copies + root_copies:
                copy.wait()
            for d in range(4):
                for j in range(RIM):
                    x = recv_x[d, :, j * BS : (j + 1) * BS].astype(f32)
                    x = jnp.where(has[d], recv_i[d, j : j + 1] * x, 0.0)
                    rim[d * RIM + j] = x.astype(bf16)

        @pl.when(a > 0)
        def _():
            for copy in copies:
                copy.wait()
            for d in range(4):
                for j in range(RIM):
                    rim[d * RIM + j] = jnp.where(has[d], recv_v[a, d, j], jnp.zeros((NVEC, BS), bf16))

        for b in range(RIM_ROWS):
            left = jnp.concatenate([rim[jnp.minimum(ptab[b, K_IN + s], RIM_ROWS - 1)] for s in range(m)], axis=1)
            acc[b] += jnp.dot(left, wtr[b * m : b * m + m].reshape(m * BS, BS), preferred_element_type=f32)
        for copy in term_copies:
            copy.wait_recv()
        alpha = jnp.where(a == 0, 1.0, 2.0).astype(f32) / HALF
        beta = jnp.where(a == 0, 0.0, 1.0).astype(f32)
        nxt = lax.rem(a + 1, 3)
        for b in range(BLK):
            total = acc[b]
            if b < RIM_ROWS:
                total = total + jnp.where(has[b // RIM], recv_t[a, b // RIM, b % RIM].astype(f32), 0.0)
            root = inv[b : b + 1]
            y = cur[b]
            new = alpha * ((y - (0.5 * root) * total) - CENTER * y) - beta * prev[b]
            prev[b] = y
            cur[b] = new
            acc[b] = root * new
        for copy in term_copies:
            copy.wait_send()
        for b in range(BLK):
            u[nxt, b] = acc[b].astype(bf16)
        return carry

    lax.fori_loop(0, 3, step, 0)

    highs = [cur[b].astype(bf16) for b in range(BLK)]
    lows = [(cur[b] - highs[b].astype(f32)).astype(bf16) for b in range(BLK)]
    stacked = jnp.concatenate([jnp.concatenate(highs, axis=1), jnp.concatenate(lows, axis=1)], axis=0)
    product = lax.dot_general(stacked, stacked, (((1,), (1,)), ((), ())), preferred_element_type=f32)
    gram = product[:NVEC, :NVEC] + product[NVEC:, NVEC:] + product[:NVEC, NVEC:] + product[NVEC:, :NVEC]
    packed = jnp.concatenate([gram[8 * g : 8 * g + 8] for g in range(4)], axis=1)

    for group, landing, sends, recvs in ((group1, ar1, s1, r1), (group2, ar2, s2, r2), (group3, ar3, s3, r3)):
        slot = {id(ar1): 0, id(ar2): 1, id(ar3): 2}[id(landing)]
        pack[slot] = packed
        sent = []
        for k, peer in enumerate(group):
            copy = pltpu.make_async_remote_copy(
                pack.at[slot], landing.at[k], sends.at[k], recvs.at[k],
                device_id=peer, device_id_type=MESH)
            copy.start()
            sent.append(copy)
        for copy in sent:
            copy.wait_recv()
        for k in range(len(group)):
            packed = packed + landing[k]
        for copy in sent:
            copy.wait_send()

    lane = lax.broadcasted_iota(i32, (NVEC, BS), 1)
    row = lax.broadcasted_iota(i32, (NVEC, BS), 0)
    moved = jnp.concatenate([pltpu.roll(packed, (96 - 32 * g) % 128, 1) for g in range(4)], axis=0)
    m = jnp.where(lane >= 96, moved, jnp.where(lax.rem(lane, 32) == row, 1.0, 0.0))
    roots = jnp.zeros((NVEC, BS), f32)
    for k in range(0, NVEC, 2):
        top = m[k : k + 1]
        low = m[k + 1 : k + 2]

        def spread(line, j):
            return jnp.broadcast_to(line[:, 96 + j : 97 + j], line.shape)

        d0 = spread(top, k)
        ratio = spread(top, k + 1) * (1.0 / d0)
        d1 = spread(low, k + 1) - spread(top, k + 1) * ratio
        second = low - ratio * top
        c0 = spread(m, k)
        c1 = spread(m, k + 1) - c0 * ratio
        roots = jnp.where(row == k, lax.rsqrt(d0), jnp.where(row == k + 1, lax.rsqrt(d1), roots))
        lower = m - c0 * (top * (1.0 / d0)) - c1 * (second * (1.0 / d1))
        m = jnp.where(row > k + 1, lower, jnp.where(row == k + 1, second, m))
    count = n_narrow * n_wide * BLK * BS
    solve = m * roots * math.sqrt(count)
    solve_ref[...] = solve


def last_kernel(solve_ref, y_ref, out_ref):
    solve = solve_ref[...]
    lane = lax.broadcasted_iota(i32, (NVEC, BS), 1)
    solve_high = solve.astype(bf16)
    solve_low = (solve - solve_high.astype(f32)).astype(bf16)
    left = jnp.where((lane >= 32) & (lane < 64), solve_low.astype(f32), solve_high.astype(f32))
    left = jnp.where(lane < 96, left, 0.0).astype(bf16)
    for b in range(y_ref.shape[0]):
        y = y_ref[b]
        high = y.astype(bf16)
        low = (y - high.astype(f32)).astype(bf16)
        right = jnp.concatenate([high, high, low, low], axis=0)
        out_ref[:, b * BS : (b + 1) * BS] = jnp.dot(left, right, preferred_element_type=f32)


def tables(pattern):
    return pl.pallas_call(
        build_tables,
        out_shape=[
            pltpu.HBM((8, N_POS), i32),
            pltpu.HBM((8, N_POS), f32),
            pltpu.HBM((NVEC, BS), i32),
            pltpu.HBM((64, K * NVEC), bf16),
        ],
        in_specs=[pl.BlockSpec(memory_space=pltpu.VMEM)],
        out_specs=[pl.BlockSpec(memory_space=pltpu.VMEM)] * 4,
        scratch_shapes=[pltpu.VMEM((NVEC, BS), f32)],
        compiler_params=pltpu.CompilerParams(vmem_limit_bytes=16 * 2**20),
        name="index_tables",
    )(pattern)


def body(start_block, weights, pattern):
    dma = pltpu.SemaphoreType.DMA
    vmem = pltpu.VMEM
    solve, final = pl.pallas_call(
        kernel,
        out_shape=[
            vmem((NVEC, BS), f32),
            vmem((BLK, NVEC, BS), f32),
        ],
        in_specs=[
            pl.BlockSpec(memory_space=pltpu.SMEM),
            pl.BlockSpec(memory_space=pltpu.SMEM),
            pl.BlockSpec(memory_space=pltpu.SMEM),
            pl.BlockSpec(memory_space=pltpu.VMEM),
            pl.BlockSpec(memory_space=pltpu.VMEM),
            pl.BlockSpec(memory_space=pl.ANY),
        ],
        out_specs=[pl.BlockSpec(memory_space=pltpu.VMEM)] * 2,
        scratch_shapes=[
            vmem((N_OWN, BS, BS), bf16),
            vmem((N_RIM, BS, BS), bf16),
            vmem((N_OWN, BS, BS), bf16),
            vmem((N_RIM, BS, BS), bf16),
            vmem((3, BLK + 1, NVEC, BS), bf16),
            vmem((RIM_ROWS, NVEC, BS), bf16),
            vmem((3, 4, RIM, NVEC, BS), bf16),
            vmem((3, 4, RIM, NVEC, BS), bf16),
            vmem((3, 4, RIM, NVEC, BS), bf16),
            vmem((4, 8, BS), bf16),
            vmem((4, 8, BS), bf16),
            vmem((BLK, NVEC, BS), f32),
            vmem((BLK, NVEC, BS), f32),
            vmem((NVEC, BS), f32),
            vmem((OWN_PAIRS, NVEC, BS), f32),
            vmem((4 * RIM_PAIRS, NVEC, BS), f32),
            vmem((3, 8, BS), f32),
            vmem((7, 8, BS), f32),
            vmem((3, 8, BS), f32),
            vmem((7, 8, BS), f32),
            vmem((K * NVEC, BS), f32),
            vmem((NVEC, BS), f32),
            vmem((4, NVEC, RIM * BS), bf16),
            vmem((4, 8, BS), f32),
            vmem((4, 8, BS), f32),
            dma((RIM_ROWS + BLK,)),
            dma((4,)),
            dma((4,)),
            dma((4,)),
            dma((4,)),
            dma((3, 4)),
            dma((3, 4)),
            dma((3, 4)),
            dma((3, 4)),
            dma((4,)),
            dma((4,)),
            dma((7,)),
            dma((7,)),
            dma((3,)),
            dma((3,)),
            dma((7,)),
            dma((7,)),
        ],
        compiler_params=pltpu.CompilerParams(
            collective_id=0, has_side_effects=True, vmem_limit_bytes=56 * 2**20
        ),
        name="filter_step",
    )(*tables(jnp.transpose(pattern, (0, 3, 1, 2)).reshape(K, 1, BLK)), start_block[0, 0], weights.reshape(BLK * K, BS, BS))
    out = pl.pallas_call(
        last_kernel,
        grid=(BLK // CHUNK,),
        out_shape=jax.ShapeDtypeStruct((NVEC, BLK * BS), f32),
        in_specs=[
            pl.BlockSpec((NVEC, BS), lambda i: (0, 0)),
            pl.BlockSpec((CHUNK, NVEC, BS), lambda i: (i, 0, 0)),
        ],
        out_specs=pl.BlockSpec((NVEC, CHUNK * BS), lambda i: (0, i)),
        compiler_params=pltpu.CompilerParams(vmem_limit_bytes=8 * 2**20),
        name="last_product",
    )(solve, final)
    return out.reshape(1, 1, NVEC, BLK * BS)


def solution(mesh):
    placed = (
        P("narrow", "wide", None, None),
        P("narrow", "wide", None, None, None, None),
        P("narrow", "wide", None, None),
    )
    return jax.shard_map(
        body, mesh=mesh, in_specs=placed, out_specs=P("narrow", "wide", None, None), check_vma=False
    )
```

```python
import math

import jax
import jax.numpy as jnp
import numpy as np
from jax import lax
from jax.experimental import pallas as pl
from jax.experimental.pallas import tpu as pltpu
from jax.sharding import PartitionSpec as P

f32 = jnp.float32
bf16 = jnp.bfloat16
i32 = jnp.int32
MESH = pl.DeviceIdType.MESH

NVEC = 32
BS = 128
K = 12
K_IN = 9
RIM = 6
BLK = 28
RIM_ROWS = 4 * RIM
LOWER = 0.3
CENTER = (2.0 + LOWER) / 2.0
HALF = (2.0 - LOWER) / 2.0
OPP = (1, 0, 3, 2)

N_OWN = RIM_ROWS * K_IN + (BLK - RIM_ROWS) * K
N_RIM = RIM_ROWS * (K - K_IN)
OWN_PAIRS = (N_OWN + BLK) // 2
RIM_PAIRS = (N_RIM // 4 + RIM) // 2
T_GROUPS = 2
Z_CHIPS = 8
Y_CHIPS = 4

N_POS = 512
OWN_POS = 2 * OWN_PAIRS
CHUNK = 7
SEND_AT = 2
OUT_PARTS = 4
SEGS = BLK + RIM_ROWS


def own_index(b):
    return b * K_IN if b < RIM_ROWS else RIM_ROWS * K_IN + (b - RIM_ROWS) * K


def build_tables(pat_ref, tab_i, tab_f, tab_p, hot_t, padded):
    tab_i[...] = jnp.zeros_like(tab_i)
    tab_f[...] = jnp.zeros_like(tab_f)
    padded[...] = jnp.full((NVEC, BS), 200.0, f32)
    for k in range(K):
        padded[k : k + 1, 0:BLK] = pat_ref[k].astype(f32)
    turned = padded[...].T[0:NVEC]
    padded[...] = jnp.full((NVEC, BS), 200.0, f32)
    padded[:, 0:NVEC] = turned
    lane = lax.broadcasted_iota(i32, (NVEC, BS), 1)
    row = lax.broadcasted_iota(i32, (NVEC, BS), 0)
    face = jnp.where(row >= RIM, 1.0, 0.0) + jnp.where(row >= 2 * RIM, 1.0, 0.0) + jnp.where(row >= 3 * RIM, 1.0, 0.0)
    t = padded[...]
    t = jnp.where((t >= BLK) & (t < 100), t + RIM * face, t)
    tab_p[...] = jnp.clip(jnp.where(t < BLK, t, t - BLK), 0.0, BLK - 1.0).astype(i32)
    rows = K * NVEC
    column = jnp.concatenate([jnp.broadcast_to(t[:, s : s + 1], (NVEC, BS)) for s in range(K)], axis=0)
    seg = lax.broadcasted_iota(i32, (rows, BS), 1).astype(f32)
    hot = jnp.where(column == seg, 1.0, 0.0)
    hot_t[...] = hot.T[0 : hot_t.shape[0]].astype(bf16)
    hot_b = hot.astype(bf16)
    lower = lax.broadcasted_iota(i32, (rows, rows), 0) > lax.broadcasted_iota(i32, (rows, rows), 1)
    before = jnp.dot(jnp.where(lower, 1.0, 0.0).astype(bf16), hot_b, preferred_element_type=f32)
    ones8 = jnp.ones((8, rows), bf16)
    count = jnp.dot(ones8, hot_b, preferred_element_type=f32)
    pairs = jnp.floor((count + 1.0) * 0.5)

    def group(e):
        total = jnp.zeros(e.shape, f32)
        for r in range(4):
            total = total + jnp.where(e >= BLK + r * RIM, 1.0, 0.0)
        return total

    e0 = lax.broadcasted_iota(i32, (BS, BS), 0)
    e1 = lax.broadcasted_iota(i32, (BS, BS), 1)
    earlier = jnp.where((e0 < e1) & (group(e0) == group(e1)), 1.0, 0.0).astype(bf16)
    e8 = lax.broadcasted_iota(i32, (8, BS), 1)
    g8 = group(e8)
    base = jnp.where(g8 > 0, OWN_PAIRS + (g8 - 1.0) * RIM_PAIRS, 0.0)
    start = jnp.dot(pairs.astype(bf16), earlier, preferred_element_type=f32) + base
    rank = jnp.sum(hot * before, axis=1, keepdims=True)
    first = jnp.sum(hot * (2.0 * start[0:1]), axis=1, keepdims=True)
    valid = column[:, 0:1] < 100.0
    pos = jnp.where(valid, rank + first, -1.0)
    place = lax.broadcasted_iota(i32, (rows, N_POS), 1).astype(f32)
    at = jnp.where(pos == place, 1.0, 0.0)
    entry = lax.broadcasted_iota(i32, (8, rows), 1)
    which = lax.broadcasted_iota(i32, (8, rows), 0)
    vals = jnp.where(which == 0, (entry & 31) + 1, jnp.where(which == 1, entry >> 5, 0)).astype(f32).astype(bf16)
    found = jnp.dot(vals, at.astype(bf16), preferred_element_type=f32)
    opens = jnp.dot(ones8, jnp.where(rank == 0.0, at, 0.0).astype(bf16), preferred_element_type=f32)
    b = found[0:1] - 1.0
    s = found[1:2]
    p = lax.broadcasted_iota(i32, (1, N_POS), 1)
    own_w = jnp.where(b < RIM_ROWS, b * K_IN + s, RIM_ROWS * K_IN + (b - RIM_ROWS) * K + s)
    rim_w = jnp.clip(b * (K - K_IN) + s - K_IN, 0.0, N_RIM - 1.0)
    w = jnp.where(p < OWN_POS, jnp.clip(own_w, 0.0, N_OWN - 1.0), rim_w)
    source = jnp.where(b >= 0, jnp.minimum(b, BLK - 1.0), float(BLK))
    end = start + pairs - 1.0
    end = jnp.where(g8 > 0, jnp.clip(end - OWN_PAIRS, 0.0, 4 * RIM_PAIRS - 1.0), jnp.clip(end, 0.0, OWN_PAIRS - 1.0))
    tab_i[0:1, :] = w.astype(i32)
    tab_i[1:2, :] = source.astype(i32)
    tab_i[2:3, 0:BS] = end[0:1].astype(i32)
    tab_f[0:1, :] = 1.0 - opens[0:1]
    tab_f[1:2, 0:BS] = jnp.where(count[0:1] > 0, 1.0, 0.0)


def kernel(
    tab_hbm, ftab_hbm, ptab_hbm, hot_hbm, start_hbm, w_hbm, solve_ref, cur,
    wo, wr, wto, wtr, u, rim, recv_v, recv_t, send_t, recv_d, send_d,
    prev, acc, inv, run_o, run_r, pack, ar1, ar2, ar3,
    sums, rowsum, recv_x, send_i, recv_i, tab, ftab, ptab, hot_t, start_ref,
    w_sem, t_sem, xs, xr, rs, rr, vs, vr, ts, tr, ds, dr, s1, r1, s2, r2, s3, r3,
):
    ni = lax.axis_index("narrow")
    wi = lax.axis_index("wide")
    n_narrow = lax.axis_size("narrow")
    n_wide = lax.axis_size("wide")
    north = lax.rem(ni + n_narrow - 1, n_narrow)
    south = lax.rem(ni + 1, n_narrow)
    west = lax.rem(wi + n_wide - 1, n_wide)
    east = lax.rem(wi + 1, n_wide)
    neighbours = ({"narrow": north}, {"narrow": south}, {"wide": west}, {"wide": east})
    has = (ni > 0, ni < n_narrow - 1, wi > 0, wi < n_wide - 1)
    wy = wi // Z_CHIPS
    wz = lax.rem(wi, Z_CHIPS)
    group1 = [{"narrow": lax.rem(ni + k, n_narrow)} for k in (4, 3, 5, 2, 6, 1, 7)]
    group2 = [{"wide": lax.rem(wi + k * Z_CHIPS, n_wide)} for k in (2, 1, 3)]
    group3 = [{"wide": wy * Z_CHIPS + lax.rem(wz + k, Z_CHIPS)} for k in (4, 3, 5, 2, 6, 1, 7)]

    barrier = pltpu.get_barrier_semaphore()
    greeted = [{"wide": west}, {"wide": east}] + group1 + group2 + group3
    for peer in greeted:
        pl.semaphore_signal(barrier, inc=1, device_id=peer, device_id_type=MESH)

    rim_copies = []
    for b in range(RIM_ROWS):
        n = K - K_IN
        rim_copies.append(pltpu.make_async_copy(
            w_hbm.at[pl.ds(b * K + K_IN, n)], wr.at[pl.ds(b * n, n)], w_sem.at[b]))
    own_copies = []
    for b in range(BLK):
        n = K_IN if b < RIM_ROWS else K
        own_copies.append(pltpu.make_async_copy(
            w_hbm.at[pl.ds(b * K, n)], wo.at[pl.ds(own_index(b), n)], w_sem.at[RIM_ROWS + b]))
    table_copies = [
        pltpu.make_async_copy(source, target, t_sem.at[k])
        for k, (source, target) in enumerate(
            ((hot_hbm, hot_t), (start_hbm, start_ref), (tab_hbm, tab), (ftab_hbm, ftab), (ptab_hbm, ptab)))
    ]
    for copy in rim_copies + table_copies[:2] + own_copies + table_copies[2:]:
        copy.start()

    for a in range(3):
        u[a, BLK] = jnp.zeros((NVEC, BS), bf16)
    sums[...] = jnp.zeros_like(sums)

    def pair_product(lhs, w, at):
        left = jnp.concatenate([lhs(tab[1, at]), lhs(tab[1, at + 1])], axis=1)
        right = jnp.concatenate([w[tab[0, at]], w[tab[0, at + 1]]], axis=0)
        return jnp.dot(left, right, preferred_element_type=f32)

    def rim_out(lhs, d, put):
        run = None
        for q in range(d * RIM_PAIRS, (d + 1) * RIM_PAIRS):
            at = OWN_POS + 2 * q
            part = pair_product(lhs, wr, at)
            run = part if run is None else run * ftab[0, at] + part
            run_r[q] = run
        for j in range(RIM):
            e = BLK + d * RIM + j
            put(d, j, (run_r[tab[2, e]] * ftab[1, e]).astype(bf16))

    def own_back(lhs):
        per = OWN_PAIRS // T_GROUPS

        def body(g, run):
            for q in range(per):
                at = g * per + q
                part = pair_product(lhs, wo, 2 * at)
                run = run * ftab[0, 2 * at] + part
                run_o[at] = run
            return run

        lax.fori_loop(0, T_GROUPS, body, jnp.zeros((NVEC, BS), f32))

    ones8 = jnp.ones((8, K * BS), bf16)

    def column_sums(w, first, n, b, s0):
        wide = jnp.concatenate([w[first + s] for s in range(n)], axis=1)
        total = jnp.dot(ones8[:, :BS], wide, preferred_element_type=f32)
        for s in range(n):
            at = (s0 + s) * NVEC + b
            sums[at : at + 1] = total[0:1, s * BS : (s + 1) * BS]

    def row_sums(wt, first, n):
        return jnp.dot(ones8[:, : n * BS], wt[first : first + n].reshape(n * BS, BS), preferred_element_type=f32)

    def grouped_sums():
        high = sums[...].astype(bf16)
        low = (sums[...] - high.astype(f32)).astype(bf16)
        return jnp.dot(hot_t[...], high, preferred_element_type=f32) + jnp.dot(
            hot_t[...], low, preferred_element_type=f32)

    for copy in rim_copies:
        copy.wait()
    m = K - K_IN
    for b in range(RIM_ROWS):
        for s in range(m):
            wtr[b * m + s] = wr[b * m + s].T
        column_sums(wr, b * m, m, b, K_IN)
    degree_copies = []
    start_copies = []

    def send_degree():
        for copy in table_copies[:2]:
            copy.wait()
        out = grouped_sums()
        for d in range(4):
            at = BLK + d * RIM
            send_d[d, 0:RIM] = out[at : at + RIM].astype(bf16)
        pl.semaphore_wait(barrier, len(greeted))
        for d in (2, 3, 0, 1):
            copy = pltpu.make_async_remote_copy(
                send_d.at[d], recv_d.at[OPP[d]], ds.at[d], dr.at[OPP[d]],
                device_id=neighbours[d], device_id_type=MESH)
            copy.start()
            degree_copies.append(copy)
        for d in (2, 3, 0, 1):
            copy = pltpu.make_async_remote_copy(
                start_ref.at[:, pl.ds(d * RIM * BS, RIM * BS)], recv_x.at[OPP[d]], xs.at[d], xr.at[OPP[d]],
                device_id=neighbours[d], device_id_type=MESH)
            copy.start()
            start_copies.append(copy)

    def own_row_sums(b):
        total = row_sums(wto, own_index(b), K_IN if b < RIM_ROWS else K)
        if b < RIM_ROWS:
            total = total + jnp.where(has[b // RIM], row_sums(wtr, b * m, m), 0.0)
        rowsum[b : b + 1] = total[0:1]

    rowsum[...] = jnp.ones_like(rowsum)
    send_d[...] = jnp.zeros_like(send_d)
    send_i[...] = jnp.zeros_like(send_i)
    chunks = [range(c, c + CHUNK) for c in range(0, BLK, CHUNK)]
    for c, chunk in enumerate(chunks):
        for b in chunk:
            own_copies[b].wait()
        if c == SEND_AT:
            send_degree()
        for b in chunk:
            n = K_IN if b < RIM_ROWS else K
            for s in range(n):
                wto[own_index(b) + s] = wo[own_index(b) + s].T
            column_sums(wo, own_index(b), n, b, 0)
        if c > 0:
            for b in chunks[c - 1]:
                own_row_sums(b)
    for b in chunks[-1]:
        own_row_sums(b)
    back = grouped_sums()
    degree = rowsum[...] + back[0:NVEC]
    rowsum[...] = degree
    for copy in degree_copies:
        copy.wait_recv()
    for d in range(4):
        at = d * RIM
        arrived = jnp.where(has[d], recv_d[d].astype(f32), 0.0)
        rowsum[at : at + RIM] = rowsum[at : at + RIM] + arrived[0:RIM]
    inv[...] = 1.0 / jnp.sqrt(0.5 * rowsum[...])
    for copy in table_copies[2:]:
        copy.wait()
    root_copies = []
    for d in (2, 3, 0, 1):
        send_i[d, 0:RIM] = inv[d * RIM : d * RIM + RIM]
    for d in (2, 3, 0, 1):
        copy = pltpu.make_async_remote_copy(
            send_i.at[d], recv_i.at[OPP[d]], rs.at[d], rr.at[OPP[d]],
            device_id=neighbours[d], device_id_type=MESH)
        copy.start()
        root_copies.append(copy)
    for b in range(BLK):
        x = start_ref[:, b * BS : (b + 1) * BS].astype(f32)
        cur[b] = x
        prev[b] = x
        u[0, b] = (inv[b : b + 1] * x).astype(bf16)
    for copy in degree_copies:
        copy.wait_send()
    def step(a, carry):
        copies = []
        for d in (2, 3, 0, 1):
            copies.append(pltpu.make_async_remote_copy(
                u.at[a, pl.ds(d * RIM, RIM)], recv_v.at[a, OPP[d]], vs.at[a, d], vr.at[a, OPP[d]],
                device_id=neighbours[d], device_id_type=MESH))

        @pl.when(a > 0)
        def _():
            for copy in copies:
                copy.start()

        def put_terms(d, j, value):
            send_t[a, d, j] = value

        term_copies = []
        for pair in ((2, 3), (0, 1)):
            for d in pair:
                rim_out(lambda k: u[a, k], d, put_terms)
            for d in pair:
                copy = pltpu.make_async_remote_copy(
                    send_t.at[a, d], recv_t.at[a, OPP[d]], ts.at[a, d], tr.at[a, OPP[d]],
                    device_id=neighbours[d], device_id_type=MESH)
                copy.start()
                term_copies.append(copy)
        own_back(lambda k: u[a, k])
        for b in range(BLK):
            n = K_IN if b < RIM_ROWS else K
            o = own_index(b)
            left = jnp.concatenate([u[a, ptab[b, s]] for s in range(n)], axis=1)
            ahead = jnp.dot(left, wto[o : o + n].reshape(n * BS, BS), preferred_element_type=f32)
            acc[b] = ahead + run_o[tab[2, b]]
        alpha = jnp.where(a == 0, 1.0, 2.0).astype(f32) / HALF
        beta = jnp.where(a == 0, 0.0, 1.0).astype(f32)
        nxt = lax.rem(a + 1, 3)

        def land(pair):
            mine = slice(0, 2) if pair == (2, 3) else slice(2, 4)

            @pl.when(a == 0)
            def _():
                for copy in start_copies[mine] + root_copies[mine]:
                    copy.wait()
                for d in pair:
                    for j in range(RIM):
                        x = recv_x[d, :, j * BS : (j + 1) * BS].astype(f32)
                        x = jnp.where(has[d], recv_i[d, j : j + 1] * x, 0.0)
                        rim[d * RIM + j] = x.astype(bf16)

            @pl.when(a > 0)
            def _():
                for copy in copies[mine]:
                    copy.wait()
                for d in pair:
                    for j in range(RIM):
                        rim[d * RIM + j] = jnp.where(has[d], recv_v[a, d, j], jnp.zeros((NVEC, BS), bf16))

            for d in pair:
                for b in range(d * RIM, (d + 1) * RIM):
                    left = jnp.concatenate(
                        [rim[jnp.minimum(ptab[b, K_IN + s], RIM_ROWS - 1)] for s in range(m)], axis=1)
                    acc[b] += jnp.dot(left, wtr[b * m : b * m + m].reshape(m * BS, BS), preferred_element_type=f32)

        def advance(blocks):
            for b in blocks:
                total = acc[b]
                if b < RIM_ROWS:
                    total = total + jnp.where(has[b // RIM], recv_t[a, b // RIM, b % RIM].astype(f32), 0.0)
                root = inv[b : b + 1]
                y = cur[b]
                new = alpha * ((y - (0.5 * root) * total) - CENTER * y) - beta * prev[b]
                prev[b] = y
                cur[b] = new
                u[nxt, b] = (root * new).astype(bf16)

        land((0, 1))
        land((2, 3))
        for copy in term_copies[2:]:
            copy.wait()
        advance(list(range(2 * RIM)) + list(range(RIM_ROWS, BLK)))
        for copy in term_copies[:2]:
            copy.wait()
        advance(range(2 * RIM, RIM_ROWS))
        return carry

    lax.fori_loop(0, 3, step, 0)

    highs = [cur[b].astype(bf16) for b in range(BLK)]
    lows = [(cur[b] - highs[b].astype(f32)).astype(bf16) for b in range(BLK)]
    stacked = jnp.concatenate([jnp.concatenate(highs, axis=1), jnp.concatenate(lows, axis=1)], axis=0)
    product = lax.dot_general(stacked, stacked, (((1,), (1,)), ((), ())), preferred_element_type=f32)
    gram = product[:NVEC, :NVEC] + product[NVEC:, NVEC:] + product[:NVEC, NVEC:] + product[NVEC:, :NVEC]
    packed = jnp.concatenate([gram[8 * g : 8 * g + 8] for g in range(4)], axis=1)

    for group, landing, sends, recvs in ((group1, ar1, s1, r1), (group2, ar2, s2, r2), (group3, ar3, s3, r3)):
        slot = {id(ar1): 0, id(ar2): 1, id(ar3): 2}[id(landing)]
        pack[slot] = packed
        sent = []
        for k, peer in enumerate(group):
            copy = pltpu.make_async_remote_copy(
                pack.at[slot], landing.at[k], sends.at[k], recvs.at[k],
                device_id=peer, device_id_type=MESH)
            copy.start()
            sent.append(copy)
        for copy in sent:
            copy.wait_recv()
        for k in range(len(group)):
            packed = packed + landing[k]
        for copy in sent:
            copy.wait_send()

    lane = lax.broadcasted_iota(i32, (NVEC, BS), 1)
    row = lax.broadcasted_iota(i32, (NVEC, BS), 0)
    moved = jnp.concatenate([pltpu.roll(packed, (96 - 32 * g) % 128, 1) for g in range(4)], axis=0)
    m = jnp.where(lane >= 96, moved, jnp.where(lax.rem(lane, 32) == row, 1.0, 0.0))
    roots = jnp.zeros((NVEC, BS), f32)
    for k in range(0, NVEC, 2):
        top = m[k : k + 1]
        low = m[k + 1 : k + 2]

        def spread(line, j):
            return jnp.broadcast_to(line[:, 96 + j : 97 + j], line.shape)

        d0 = spread(top, k)
        ratio = spread(top, k + 1) * (1.0 / d0)
        d1 = spread(low, k + 1) - spread(top, k + 1) * ratio
        second = low - ratio * top
        c0 = spread(m, k)
        c1 = spread(m, k + 1) - c0 * ratio
        roots = jnp.where(row == k, lax.rsqrt(d0), jnp.where(row == k + 1, lax.rsqrt(d1), roots))
        lower = m - c0 * (top * (1.0 / d0)) - c1 * (second * (1.0 / d1))
        m = jnp.where(row > k + 1, lower, jnp.where(row == k + 1, second, m))
    count = n_narrow * n_wide * BLK * BS
    solve = m * roots * math.sqrt(count)
    solve_ref[...] = solve


def last_kernel(solve_ref, y_ref, out_hbm, held, sem):
    solve = solve_ref[...]
    lane = lax.broadcasted_iota(i32, (NVEC, BS), 1)
    solve_high = solve.astype(bf16)
    solve_low = (solve - solve_high.astype(f32)).astype(bf16)
    left = jnp.where((lane >= 32) & (lane < 64), solve_low.astype(f32), solve_high.astype(f32))
    left = jnp.where(lane < 96, left, 0.0).astype(bf16)
    copies = []
    for c in range(OUT_PARTS):
        per = BLK // OUT_PARTS
        for b in range(c * per, (c + 1) * per):
            y = y_ref[b]
            high = y.astype(bf16)
            low = (y - high.astype(f32)).astype(bf16)
            right = jnp.concatenate([high, high, low, low], axis=0)
            held[:, b * BS : (b + 1) * BS] = jnp.dot(left, right, preferred_element_type=f32)
        part = pl.ds(c * per * BS, per * BS)
        copies.append(pltpu.make_async_copy(held.at[:, part], out_hbm.at[:, part], sem.at[c]))
        copies[-1].start()
    for copy in copies:
        copy.wait()


def tables(pattern):
    return pl.pallas_call(
        build_tables,
        out_shape=[
            pltpu.HBM((8, N_POS), i32),
            pltpu.HBM((8, N_POS), f32),
            pltpu.HBM((NVEC, BS), i32),
            pltpu.HBM((64, K * NVEC), bf16),
        ],
        in_specs=[pl.BlockSpec(memory_space=pltpu.VMEM)],
        out_specs=[pl.BlockSpec(memory_space=pltpu.VMEM)] * 4,
        scratch_shapes=[pltpu.VMEM((NVEC, BS), f32)],
        compiler_params=pltpu.CompilerParams(vmem_limit_bytes=16 * 2**20),
        name="index_tables",
    )(pattern)


def body(start_block, weights, pattern):
    dma = pltpu.SemaphoreType.DMA
    vmem = pltpu.VMEM
    solve, final = pl.pallas_call(
        kernel,
        out_shape=[
            vmem((NVEC, BS), f32),
            vmem((BLK, NVEC, BS), f32),
        ],
        in_specs=[
            pl.BlockSpec(memory_space=pl.ANY),
        ]
        * 6,
        out_specs=[pl.BlockSpec(memory_space=pltpu.VMEM)] * 2,
        scratch_shapes=[
            vmem((N_OWN, BS, BS), bf16),
            vmem((N_RIM, BS, BS), bf16),
            vmem((N_OWN, BS, BS), bf16),
            vmem((N_RIM, BS, BS), bf16),
            vmem((3, BLK + 1, NVEC, BS), bf16),
            vmem((RIM_ROWS, NVEC, BS), bf16),
            vmem((3, 4, RIM, NVEC, BS), bf16),
            vmem((3, 4, RIM, NVEC, BS), bf16),
            vmem((3, 4, RIM, NVEC, BS), bf16),
            vmem((4, 8, BS), bf16),
            vmem((4, 8, BS), bf16),
            vmem((BLK, NVEC, BS), f32),
            vmem((BLK, NVEC, BS), f32),
            vmem((NVEC, BS), f32),
            vmem((OWN_PAIRS, NVEC, BS), f32),
            vmem((4 * RIM_PAIRS, NVEC, BS), f32),
            vmem((3, 8, BS), f32),
            vmem((7, 8, BS), f32),
            vmem((3, 8, BS), f32),
            vmem((7, 8, BS), f32),
            vmem((K * NVEC, BS), f32),
            vmem((NVEC, BS), f32),
            vmem((4, NVEC, RIM * BS), bf16),
            vmem((4, 8, BS), f32),
            vmem((4, 8, BS), f32),
            pltpu.SMEM((8, N_POS), i32),
            pltpu.SMEM((8, N_POS), f32),
            pltpu.SMEM((NVEC, BS), i32),
            vmem((64, K * NVEC), bf16),
            vmem((NVEC, BLK * BS), bf16),
            dma((RIM_ROWS + BLK,)),
            dma((5,)),
            dma((4,)),
            dma((4,)),
            dma((4,)),
            dma((4,)),
            dma((3, 4)),
            dma((3, 4)),
            dma((3, 4)),
            dma((3, 4)),
            dma((4,)),
            dma((4,)),
            dma((7,)),
            dma((7,)),
            dma((3,)),
            dma((3,)),
            dma((7,)),
            dma((7,)),
        ],
        compiler_params=pltpu.CompilerParams(
            collective_id=0, has_side_effects=True, vmem_limit_bytes=56 * 2**20
        ),
        name="filter_step",
    )(*tables(jnp.transpose(pattern, (0, 3, 1, 2)).reshape(K, 1, BLK)), start_block[0, 0], weights.reshape(BLK * K, BS, BS))
    out = pl.pallas_call(
        last_kernel,
        out_shape=jax.ShapeDtypeStruct((NVEC, BLK * BS), f32),
        in_specs=[pl.BlockSpec(memory_space=pltpu.VMEM)] * 2,
        out_specs=pl.BlockSpec(memory_space=pl.ANY),
        scratch_shapes=[vmem((NVEC, BLK * BS), f32), dma((OUT_PARTS,))],
        compiler_params=pltpu.CompilerParams(vmem_limit_bytes=8 * 2**20),
        name="last_product",
    )(solve, final)
    return out.reshape(1, 1, NVEC, BLK * BS)


def solution(mesh):
    placed = (
        P("narrow", "wide", None, None),
        P("narrow", "wide", None, None, None, None),
        P("narrow", "wide", None, None),
    )
    return jax.shard_map(
        body, mesh=mesh, in_specs=placed, out_specs=P("narrow", "wide", None, None), check_vma=False
    )
```

```python
import math

import jax
import jax.numpy as jnp
import numpy as np
from jax import lax
from jax.experimental import pallas as pl
from jax.experimental.pallas import tpu as pltpu
from jax.sharding import PartitionSpec as P

f32 = jnp.float32
bf16 = jnp.bfloat16
i32 = jnp.int32
MESH = pl.DeviceIdType.MESH

NVEC = 32
BS = 128
K = 12
K_IN = 9
RIM = 6
BLK = 28
RIM_ROWS = 4 * RIM
LOWER = 0.3
CENTER = (2.0 + LOWER) / 2.0
HALF = (2.0 - LOWER) / 2.0
OPP = (1, 0, 3, 2)

N_OWN = RIM_ROWS * K_IN + (BLK - RIM_ROWS) * K
N_RIM = RIM_ROWS * (K - K_IN)
OWN_PAIRS = (N_OWN + BLK) // 2
RIM_PAIRS = (N_RIM // 4 + RIM) // 2
T_GROUPS = 2
Z_CHIPS = 8
Y_CHIPS = 4

N_POS = 512
OWN_POS = 2 * OWN_PAIRS
CHUNK = 7
SEND_AT = 2
OUT_PARTS = 4
SEGS = BLK + RIM_ROWS


def own_index(b):
    return b * K_IN if b < RIM_ROWS else RIM_ROWS * K_IN + (b - RIM_ROWS) * K


def build_tables(pat_ref, tab_i, tab_f, tab_p, hot_t, padded):
    tab_i[...] = jnp.zeros_like(tab_i)
    tab_f[...] = jnp.zeros_like(tab_f)
    padded[...] = jnp.full((NVEC, BS), 200.0, f32)
    for k in range(K):
        padded[k : k + 1, 0:BLK] = pat_ref[k].astype(f32)
    turned = padded[...].T[0:NVEC]
    padded[...] = jnp.full((NVEC, BS), 200.0, f32)
    padded[:, 0:NVEC] = turned
    lane = lax.broadcasted_iota(i32, (NVEC, BS), 1)
    row = lax.broadcasted_iota(i32, (NVEC, BS), 0)
    face = jnp.where(row >= RIM, 1.0, 0.0) + jnp.where(row >= 2 * RIM, 1.0, 0.0) + jnp.where(row >= 3 * RIM, 1.0, 0.0)
    t = padded[...]
    t = jnp.where((t >= BLK) & (t < 100), t + RIM * face, t)
    tab_p[...] = jnp.clip(jnp.where(t < BLK, t, t - BLK).astype(i32), 0, BLK - 1)
    rows = K * NVEC
    column = jnp.concatenate([jnp.broadcast_to(t[:, s : s + 1], (NVEC, BS)) for s in range(K)], axis=0)
    seg = lax.broadcasted_iota(i32, (rows, BS), 1).astype(f32)
    hot = jnp.where(column == seg, 1.0, 0.0)
    hot_t[...] = hot.T[0 : hot_t.shape[0]].astype(bf16)
    hot_b = hot.astype(bf16)
    lower = lax.broadcasted_iota(i32, (rows, rows), 0) > lax.broadcasted_iota(i32, (rows, rows), 1)
    before = jnp.dot(jnp.where(lower, 1.0, 0.0).astype(bf16), hot_b, preferred_element_type=f32)
    ones8 = jnp.ones((8, rows), bf16)
    count = jnp.dot(ones8, hot_b, preferred_element_type=f32)
    pairs = jnp.floor((count + 1.0) * 0.5)

    def group(e):
        total = jnp.zeros(e.shape, f32)
        for r in range(4):
            total = total + jnp.where(e >= BLK + r * RIM, 1.0, 0.0)
        return total

    e0 = lax.broadcasted_iota(i32, (BS, BS), 0)
    e1 = lax.broadcasted_iota(i32, (BS, BS), 1)
    earlier = jnp.where((e0 < e1) & (group(e0) == group(e1)), 1.0, 0.0).astype(bf16)
    e8 = lax.broadcasted_iota(i32, (8, BS), 1)
    g8 = group(e8)
    base = jnp.where(g8 > 0, OWN_PAIRS + (g8 - 1.0) * RIM_PAIRS, 0.0)
    start = jnp.dot(pairs.astype(bf16), earlier, preferred_element_type=f32) + base
    rank = jnp.sum(hot * before, axis=1, keepdims=True)
    first = jnp.sum(hot * (2.0 * start[0:1]), axis=1, keepdims=True)
    valid = column[:, 0:1] < 100.0
    pos = jnp.where(valid, rank + first, -1.0)
    place = lax.broadcasted_iota(i32, (rows, N_POS), 1).astype(f32)
    at = jnp.where(pos == place, 1.0, 0.0)
    entry = lax.broadcasted_iota(i32, (8, rows), 1)
    which = lax.broadcasted_iota(i32, (8, rows), 0)
    vals = jnp.where(which == 0, (entry & 31) + 1, jnp.where(which == 1, entry >> 5, 0)).astype(f32).astype(bf16)
    found = jnp.dot(vals, at.astype(bf16), preferred_element_type=f32)
    opens = jnp.dot(ones8, jnp.where(rank == 0.0, at, 0.0).astype(bf16), preferred_element_type=f32)
    b = found[0:1] - 1.0
    s = found[1:2]
    p = lax.broadcasted_iota(i32, (1, N_POS), 1)
    own_w = jnp.where(b < RIM_ROWS, b * K_IN + s, RIM_ROWS * K_IN + (b - RIM_ROWS) * K + s)
    rim_w = jnp.clip(b * (K - K_IN) + s - K_IN, 0.0, N_RIM - 1.0)
    w = jnp.where(p < OWN_POS, jnp.clip(own_w, 0.0, N_OWN - 1.0), rim_w)
    source = jnp.where(b >= 0, jnp.minimum(b, BLK - 1.0), float(BLK))
    end = start + pairs - 1.0
    end = jnp.where(g8 > 0, jnp.clip(end - OWN_PAIRS, 0.0, 4 * RIM_PAIRS - 1.0), jnp.clip(end, 0.0, OWN_PAIRS - 1.0))
    tab_i[0:1, :] = jnp.clip(w.astype(i32), 0, jnp.where(p < OWN_POS, N_OWN - 1, N_RIM - 1))
    tab_i[1:2, :] = jnp.clip(source.astype(i32), 0, BLK)
    limit = jnp.where(e8[0:1] >= BLK, 4 * RIM_PAIRS - 1, OWN_PAIRS - 1)
    tab_i[2:3, 0:BS] = jnp.clip(end[0:1].astype(i32), 0, limit)
    tab_f[0:1, :] = 1.0 - opens[0:1]
    tab_f[1:2, 0:BS] = jnp.where(count[0:1] > 0, 1.0, 0.0)


def kernel(
    pat_ref, start_hbm, w_hbm, solve_ref, cur,
    wo, wr, wto, wtr, u, rim, recv_v, recv_t, send_t, recv_d, send_d,
    prev, acc, inv, run_o, run_r, pack, ar1, ar2, ar3,
    sums, rowsum, recv_x, send_i, recv_i, tab, ftab, ptab, hot_t, start_ref, tab_i, tab_f, tab_p, padded,
    w_sem, t_sem, xs, xr, rs, rr, vs, vr, ts, tr, ds, dr, s1, r1, s2, r2, s3, r3,
):
    ni = lax.axis_index("narrow")
    wi = lax.axis_index("wide")
    n_narrow = lax.axis_size("narrow")
    n_wide = lax.axis_size("wide")
    north = lax.rem(ni + n_narrow - 1, n_narrow)
    south = lax.rem(ni + 1, n_narrow)
    west = lax.rem(wi + n_wide - 1, n_wide)
    east = lax.rem(wi + 1, n_wide)
    neighbours = ({"narrow": north}, {"narrow": south}, {"wide": west}, {"wide": east})
    has = (ni > 0, ni < n_narrow - 1, wi > 0, wi < n_wide - 1)
    wy = wi // Z_CHIPS
    wz = lax.rem(wi, Z_CHIPS)
    group1 = [{"narrow": lax.rem(ni + k, n_narrow)} for k in (4, 3, 5, 2, 6, 1, 7)]
    group2 = [{"wide": lax.rem(wi + k * Z_CHIPS, n_wide)} for k in (2, 1, 3)]
    group3 = [{"wide": wy * Z_CHIPS + lax.rem(wz + k, Z_CHIPS)} for k in (4, 3, 5, 2, 6, 1, 7)]

    barrier = pltpu.get_barrier_semaphore()
    greeted = [{"wide": west}, {"wide": east}] + group1 + group2 + group3
    for peer in greeted:
        pl.semaphore_signal(barrier, inc=1, device_id=peer, device_id_type=MESH)

    rim_copies = []
    for b in range(RIM_ROWS):
        n = K - K_IN
        rim_copies.append(pltpu.make_async_copy(
            w_hbm.at[pl.ds(b * K + K_IN, n)], wr.at[pl.ds(b * n, n)], w_sem.at[b]))
    own_copies = []
    for b in range(BLK):
        n = K_IN if b < RIM_ROWS else K
        own_copies.append(pltpu.make_async_copy(
            w_hbm.at[pl.ds(b * K, n)], wo.at[pl.ds(own_index(b), n)], w_sem.at[RIM_ROWS + b]))
    start_copy = pltpu.make_async_copy(start_hbm, start_ref, t_sem.at[3])
    for copy in rim_copies + [start_copy] + own_copies:
        copy.start()
    build_tables(pat_ref, tab_i, tab_f, tab_p, hot_t, padded)
    table_copies = [
        pltpu.make_async_copy(source, target, t_sem.at[k])
        for k, (source, target) in enumerate(((tab_i, tab), (tab_f, ftab), (tab_p, ptab)))
    ]
    for copy in table_copies:
        copy.start()

    for a in range(3):
        u[a, BLK] = jnp.zeros((NVEC, BS), bf16)
    sums[...] = jnp.zeros_like(sums)

    def pair_product(lhs, w, at):
        left = jnp.concatenate([lhs(tab[1, at]), lhs(tab[1, at + 1])], axis=1)
        right = jnp.concatenate([w[tab[0, at]], w[tab[0, at + 1]]], axis=0)
        return jnp.dot(left, right, preferred_element_type=f32)

    def rim_out(lhs, d, put):
        run = None
        for q in range(d * RIM_PAIRS, (d + 1) * RIM_PAIRS):
            at = OWN_POS + 2 * q
            part = pair_product(lhs, wr, at)
            run = part if run is None else run * ftab[0, at] + part
            run_r[q] = run
        for j in range(RIM):
            e = BLK + d * RIM + j
            put(d, j, (run_r[tab[2, e]] * ftab[1, e]).astype(bf16))

    def own_back(lhs):
        per = OWN_PAIRS // T_GROUPS

        def body(g, run):
            for q in range(per):
                at = g * per + q
                part = pair_product(lhs, wo, 2 * at)
                run = run * ftab[0, 2 * at] + part
                run_o[at] = run
            return run

        lax.fori_loop(0, T_GROUPS, body, jnp.zeros((NVEC, BS), f32))

    ones8 = jnp.ones((8, K * BS), bf16)

    def column_sums(w, first, n, b, s0):
        wide = jnp.concatenate([w[first + s] for s in range(n)], axis=1)
        total = jnp.dot(ones8[:, :BS], wide, preferred_element_type=f32)
        for s in range(n):
            at = (s0 + s) * NVEC + b
            sums[at : at + 1] = total[0:1, s * BS : (s + 1) * BS]

    def row_sums(wt, first, n):
        return jnp.dot(ones8[:, : n * BS], wt[first : first + n].reshape(n * BS, BS), preferred_element_type=f32)

    def grouped_sums():
        high = sums[...].astype(bf16)
        low = (sums[...] - high.astype(f32)).astype(bf16)
        return jnp.dot(hot_t[...], high, preferred_element_type=f32) + jnp.dot(
            hot_t[...], low, preferred_element_type=f32)

    for copy in rim_copies:
        copy.wait()
    m = K - K_IN
    for b in range(RIM_ROWS):
        for s in range(m):
            wtr[b * m + s] = wr[b * m + s].T
        column_sums(wr, b * m, m, b, K_IN)
    degree_copies = []
    start_copies = []

    def send_degree():
        start_copy.wait()
        out = grouped_sums()
        for d in range(4):
            at = BLK + d * RIM
            send_d[d, 0:RIM] = out[at : at + RIM].astype(bf16)
        pl.semaphore_wait(barrier, len(greeted))
        for d in (2, 3, 0, 1):
            copy = pltpu.make_async_remote_copy(
                send_d.at[d], recv_d.at[OPP[d]], ds.at[d], dr.at[OPP[d]],
                device_id=neighbours[d], device_id_type=MESH)
            copy.start()
            degree_copies.append(copy)
        for d in (2, 3, 0, 1):
            copy = pltpu.make_async_remote_copy(
                start_ref.at[:, pl.ds(d * RIM * BS, RIM * BS)], recv_x.at[OPP[d]], xs.at[d], xr.at[OPP[d]],
                device_id=neighbours[d], device_id_type=MESH)
            copy.start()
            start_copies.append(copy)

    def own_row_sums(b):
        total = row_sums(wto, own_index(b), K_IN if b < RIM_ROWS else K)
        if b < RIM_ROWS:
            total = total + jnp.where(has[b // RIM], row_sums(wtr, b * m, m), 0.0)
        rowsum[b : b + 1] = total[0:1]

    rowsum[...] = jnp.ones_like(rowsum)
    send_d[...] = jnp.zeros_like(send_d)
    send_i[...] = jnp.zeros_like(send_i)
    chunks = [range(c, c + CHUNK) for c in range(0, BLK, CHUNK)]
    for c, chunk in enumerate(chunks):
        for b in chunk:
            own_copies[b].wait()
        if c == SEND_AT:
            send_degree()
        for b in chunk:
            n = K_IN if b < RIM_ROWS else K
            for s in range(n):
                wto[own_index(b) + s] = wo[own_index(b) + s].T
            column_sums(wo, own_index(b), n, b, 0)
        if c > 0:
            for b in chunks[c - 1]:
                own_row_sums(b)
    for b in chunks[-1]:
        own_row_sums(b)
    back = grouped_sums()
    degree = rowsum[...] + back[0:NVEC]
    rowsum[...] = degree
    for copy in degree_copies:
        copy.wait_recv()
    for d in range(4):
        at = d * RIM
        arrived = jnp.where(has[d], recv_d[d].astype(f32), 0.0)
        rowsum[at : at + RIM] = rowsum[at : at + RIM] + arrived[0:RIM]
    inv[...] = 1.0 / jnp.sqrt(0.5 * rowsum[...])
    for copy in table_copies:
        copy.wait()
    root_copies = []
    for d in (2, 3, 0, 1):
        send_i[d, 0:RIM] = inv[d * RIM : d * RIM + RIM]
    for d in (2, 3, 0, 1):
        copy = pltpu.make_async_remote_copy(
            send_i.at[d], recv_i.at[OPP[d]], rs.at[d], rr.at[OPP[d]],
            device_id=neighbours[d], device_id_type=MESH)
        copy.start()
        root_copies.append(copy)
    for b in range(BLK):
        x = start_ref[:, b * BS : (b + 1) * BS].astype(f32)
        cur[b] = x
        prev[b] = x
        u[0, b] = (inv[b : b + 1] * x).astype(bf16)
    for copy in degree_copies:
        copy.wait_send()
    def step(a, carry):
        copies = []
        for d in (2, 3, 0, 1):
            copies.append(pltpu.make_async_remote_copy(
                u.at[a, pl.ds(d * RIM, RIM)], recv_v.at[a, OPP[d]], vs.at[a, d], vr.at[a, OPP[d]],
                device_id=neighbours[d], device_id_type=MESH))

        @pl.when(a > 0)
        def _():
            for copy in copies:
                copy.start()

        def put_terms(d, j, value):
            send_t[a, d, j] = value

        term_copies = []
        for pair in ((2, 3), (0, 1)):
            for d in pair:
                rim_out(lambda k: u[a, k], d, put_terms)
            for d in pair:
                copy = pltpu.make_async_remote_copy(
                    send_t.at[a, d], recv_t.at[a, OPP[d]], ts.at[a, d], tr.at[a, OPP[d]],
                    device_id=neighbours[d], device_id_type=MESH)
                copy.start()
                term_copies.append(copy)
        own_back(lambda k: u[a, k])
        for b in range(BLK):
            n = K_IN if b < RIM_ROWS else K
            o = own_index(b)
            left = jnp.concatenate([u[a, ptab[b, s]] for s in range(n)], axis=1)
            ahead = jnp.dot(left, wto[o : o + n].reshape(n * BS, BS), preferred_element_type=f32)
            acc[b] = ahead + run_o[tab[2, b]]
        alpha = jnp.where(a == 0, 1.0, 2.0).astype(f32) / HALF
        beta = jnp.where(a == 0, 0.0, 1.0).astype(f32)
        nxt = lax.rem(a + 1, 3)

        def land(pair):
            mine = slice(0, 2) if pair == (2, 3) else slice(2, 4)

            @pl.when(a == 0)
            def _():
                for copy in start_copies[mine] + root_copies[mine]:
                    copy.wait()
                for d in pair:
                    for j in range(RIM):
                        x = recv_x[d, :, j * BS : (j + 1) * BS].astype(f32)
                        x = jnp.where(has[d], recv_i[d, j : j + 1] * x, 0.0)
                        rim[d * RIM + j] = x.astype(bf16)

            @pl.when(a > 0)
            def _():
                for copy in copies[mine]:
                    copy.wait()
                for d in pair:
                    for j in range(RIM):
                        rim[d * RIM + j] = jnp.where(has[d], recv_v[a, d, j], jnp.zeros((NVEC, BS), bf16))

            for d in pair:
                for b in range(d * RIM, (d + 1) * RIM):
                    left = jnp.concatenate(
                        [rim[jnp.minimum(ptab[b, K_IN + s], RIM_ROWS - 1)] for s in range(m)], axis=1)
                    acc[b] += jnp.dot(left, wtr[b * m : b * m + m].reshape(m * BS, BS), preferred_element_type=f32)

        def advance(blocks):
            for b in blocks:
                total = acc[b]
                if b < RIM_ROWS:
                    total = total + jnp.where(has[b // RIM], recv_t[a, b // RIM, b % RIM].astype(f32), 0.0)
                root = inv[b : b + 1]
                y = cur[b]
                new = alpha * ((y - (0.5 * root) * total) - CENTER * y) - beta * prev[b]
                prev[b] = y
                cur[b] = new
                u[nxt, b] = (root * new).astype(bf16)

        land((0, 1))
        land((2, 3))
        for copy in term_copies[2:]:
            copy.wait()
        advance(list(range(2 * RIM)) + list(range(RIM_ROWS, BLK)))
        for copy in term_copies[:2]:
            copy.wait()
        advance(range(2 * RIM, RIM_ROWS))
        return carry

    lax.fori_loop(0, 3, step, 0)

    highs = [cur[b].astype(bf16) for b in range(BLK)]
    lows = [(cur[b] - highs[b].astype(f32)).astype(bf16) for b in range(BLK)]
    stacked = jnp.concatenate([jnp.concatenate(highs, axis=1), jnp.concatenate(lows, axis=1)], axis=0)
    product = lax.dot_general(stacked, stacked, (((1,), (1,)), ((), ())), preferred_element_type=f32)
    gram = product[:NVEC, :NVEC] + product[NVEC:, NVEC:] + product[:NVEC, NVEC:] + product[NVEC:, :NVEC]
    packed = jnp.concatenate([gram[8 * g : 8 * g + 8] for g in range(4)], axis=1)

    for group, landing, sends, recvs in ((group1, ar1, s1, r1), (group2, ar2, s2, r2), (group3, ar3, s3, r3)):
        slot = {id(ar1): 0, id(ar2): 1, id(ar3): 2}[id(landing)]
        pack[slot] = packed
        sent = []
        for k, peer in enumerate(group):
            copy = pltpu.make_async_remote_copy(
                pack.at[slot], landing.at[k], sends.at[k], recvs.at[k],
                device_id=peer, device_id_type=MESH)
            copy.start()
            sent.append(copy)
        for copy in sent:
            copy.wait_recv()
        for k in range(len(group)):
            packed = packed + landing[k]
        for copy in sent:
            copy.wait_send()

    lane = lax.broadcasted_iota(i32, (NVEC, BS), 1)
    row = lax.broadcasted_iota(i32, (NVEC, BS), 0)
    moved = jnp.concatenate([pltpu.roll(packed, (96 - 32 * g) % 128, 1) for g in range(4)], axis=0)
    m = jnp.where(lane >= 96, moved, jnp.where(lax.rem(lane, 32) == row, 1.0, 0.0))
    roots = jnp.zeros((NVEC, BS), f32)
    for k in range(0, NVEC, 2):
        top = m[k : k + 1]
        low = m[k + 1 : k + 2]

        def spread(line, j):
            return jnp.broadcast_to(line[:, 96 + j : 97 + j], line.shape)

        d0 = spread(top, k)
        ratio = spread(top, k + 1) * (1.0 / d0)
        d1 = spread(low, k + 1) - spread(top, k + 1) * ratio
        second = low - ratio * top
        c0 = spread(m, k)
        c1 = spread(m, k + 1) - c0 * ratio
        roots = jnp.where(row == k, lax.rsqrt(d0), jnp.where(row == k + 1, lax.rsqrt(d1), roots))
        lower = m - c0 * (top * (1.0 / d0)) - c1 * (second * (1.0 / d1))
        m = jnp.where(row > k + 1, lower, jnp.where(row == k + 1, second, m))
    count = n_narrow * n_wide * BLK * BS
    solve = m * roots * math.sqrt(count)
    solve_ref[...] = solve


def last_kernel(solve_ref, y_ref, out_hbm, held, sem):
    solve = solve_ref[...]
    lane = lax.broadcasted_iota(i32, (NVEC, BS), 1)
    solve_high = solve.astype(bf16)
    solve_low = (solve - solve_high.astype(f32)).astype(bf16)
    left = jnp.where((lane >= 32) & (lane < 64), solve_low.astype(f32), solve_high.astype(f32))
    left = jnp.where(lane < 96, left, 0.0).astype(bf16)
    copies = []
    for c in range(OUT_PARTS):
        per = BLK // OUT_PARTS
        for b in range(c * per, (c + 1) * per):
            y = y_ref[b]
            high = y.astype(bf16)
            low = (y - high.astype(f32)).astype(bf16)
            right = jnp.concatenate([high, high, low, low], axis=0)
            held[:, b * BS : (b + 1) * BS] = jnp.dot(left, right, preferred_element_type=f32)
        part = pl.ds(c * per * BS, per * BS)
        copies.append(pltpu.make_async_copy(held.at[:, part], out_hbm.at[:, part], sem.at[c]))
        copies[-1].start()
    for copy in copies:
        copy.wait()


def body(start_block, weights, pattern):
    dma = pltpu.SemaphoreType.DMA
    vmem = pltpu.VMEM
    solve, final = pl.pallas_call(
        kernel,
        out_shape=[
            vmem((NVEC, BS), f32),
            vmem((BLK, NVEC, BS), f32),
        ],
        in_specs=[
            pl.BlockSpec(memory_space=pltpu.VMEM),
            pl.BlockSpec(memory_space=pl.ANY),
            pl.BlockSpec(memory_space=pl.ANY),
        ],
        out_specs=[pl.BlockSpec(memory_space=pltpu.VMEM)] * 2,
        scratch_shapes=[
            vmem((N_OWN, BS, BS), bf16),
            vmem((N_RIM, BS, BS), bf16),
            vmem((N_OWN, BS, BS), bf16),
            vmem((N_RIM, BS, BS), bf16),
            vmem((3, BLK + 1, NVEC, BS), bf16),
            vmem((RIM_ROWS, NVEC, BS), bf16),
            vmem((3, 4, RIM, NVEC, BS), bf16),
            vmem((3, 4, RIM, NVEC, BS), bf16),
            vmem((3, 4, RIM, NVEC, BS), bf16),
            vmem((4, 8, BS), bf16),
            vmem((4, 8, BS), bf16),
            vmem((BLK, NVEC, BS), f32),
            vmem((BLK, NVEC, BS), f32),
            vmem((NVEC, BS), f32),
            vmem((OWN_PAIRS, NVEC, BS), f32),
            vmem((4 * RIM_PAIRS, NVEC, BS), f32),
            vmem((3, 8, BS), f32),
            vmem((7, 8, BS), f32),
            vmem((3, 8, BS), f32),
            vmem((7, 8, BS), f32),
            vmem((K * NVEC, BS), f32),
            vmem((NVEC, BS), f32),
            vmem((4, NVEC, RIM * BS), bf16),
            vmem((4, 8, BS), f32),
            vmem((4, 8, BS), f32),
            pltpu.SMEM((8, N_POS), i32),
            pltpu.SMEM((8, N_POS), f32),
            pltpu.SMEM((NVEC, BS), i32),
            vmem((64, K * NVEC), bf16),
            vmem((NVEC, BLK * BS), bf16),
            vmem((8, N_POS), i32),
            vmem((8, N_POS), f32),
            vmem((NVEC, BS), i32),
            vmem((NVEC, BS), f32),
            dma((RIM_ROWS + BLK,)),
            dma((4,)),
            dma((4,)),
            dma((4,)),
            dma((4,)),
            dma((4,)),
            dma((3, 4)),
            dma((3, 4)),
            dma((3, 4)),
            dma((3, 4)),
            dma((4,)),
            dma((4,)),
            dma((7,)),
            dma((7,)),
            dma((3,)),
            dma((3,)),
            dma((7,)),
            dma((7,)),
        ],
        compiler_params=pltpu.CompilerParams(
            collective_id=0, has_side_effects=True, vmem_limit_bytes=56 * 2**20
        ),
        name="filter_step",
    )(jnp.transpose(pattern, (0, 3, 1, 2)).reshape(K, 1, BLK), start_block[0, 0], weights.reshape(BLK * K, BS, BS))
    out = pl.pallas_call(
        last_kernel,
        out_shape=jax.ShapeDtypeStruct((NVEC, BLK * BS), f32),
        in_specs=[pl.BlockSpec(memory_space=pltpu.VMEM)] * 2,
        out_specs=pl.BlockSpec(memory_space=pl.ANY),
        scratch_shapes=[vmem((NVEC, BLK * BS), f32), dma((OUT_PARTS,))],
        compiler_params=pltpu.CompilerParams(vmem_limit_bytes=8 * 2**20),
        name="last_product",
    )(solve, final)
    return out.reshape(1, 1, NVEC, BLK * BS)


def solution(mesh):
    placed = (
        P("narrow", "wide", None, None),
        P("narrow", "wide", None, None, None, None),
        P("narrow", "wide", None, None),
    )
    return jax.shard_map(
        body, mesh=mesh, in_specs=placed, out_specs=P("narrow", "wide", None, None), check_vma=False
    )
```

```python
import math

import jax
import jax.numpy as jnp
import numpy as np
from jax import lax
from jax.experimental import pallas as pl
from jax.experimental.pallas import tpu as pltpu
from jax.sharding import PartitionSpec as P

f32 = jnp.float32
bf16 = jnp.bfloat16
i32 = jnp.int32
MESH = pl.DeviceIdType.MESH

NVEC = 32
BS = 128
K = 12
K_IN = 9
RIM = 6
BLK = 28
RIM_ROWS = 4 * RIM
LOWER = 0.3
CENTER = (2.0 + LOWER) / 2.0
HALF = (2.0 - LOWER) / 2.0
OPP = (1, 0, 3, 2)

N_OWN = RIM_ROWS * K_IN + (BLK - RIM_ROWS) * K
N_RIM = RIM_ROWS * (K - K_IN)
OWN_PAIRS = (N_OWN + BLK) // 2
RIM_PAIRS = (N_RIM // 4 + RIM) // 2
T_GROUPS = 1
Z_CHIPS = 8
Y_CHIPS = 4

N_POS = 512
OWN_POS = 2 * OWN_PAIRS
CHUNK = 7
SEND_AT = 2
OUT_PARTS = 4
SEGS = BLK + RIM_ROWS


def own_index(b):
    return b * K_IN if b < RIM_ROWS else RIM_ROWS * K_IN + (b - RIM_ROWS) * K


def build_tables(pat_ref, tab_i, tab_f, tab_p, hot_t, padded):
    tab_i[...] = jnp.zeros_like(tab_i)
    tab_f[...] = jnp.zeros_like(tab_f)
    padded[...] = jnp.full((NVEC, BS), 200.0, f32)
    for k in range(K):
        padded[k : k + 1, 0:BLK] = pat_ref[k].astype(f32)
    turned = padded[...].T[0:NVEC]
    padded[...] = jnp.full((NVEC, BS), 200.0, f32)
    padded[:, 0:NVEC] = turned
    lane = lax.broadcasted_iota(i32, (NVEC, BS), 1)
    row = lax.broadcasted_iota(i32, (NVEC, BS), 0)
    face = jnp.where(row >= RIM, 1.0, 0.0) + jnp.where(row >= 2 * RIM, 1.0, 0.0) + jnp.where(row >= 3 * RIM, 1.0, 0.0)
    t = padded[...]
    t = jnp.where((t >= BLK) & (t < 100), t + RIM * face, t)
    tab_p[...] = jnp.clip(jnp.where(t < BLK, t, t - BLK).astype(i32), 0, BLK - 1)
    rows = K * NVEC
    column = jnp.concatenate([jnp.broadcast_to(t[:, s : s + 1], (NVEC, BS)) for s in range(K)], axis=0)
    seg = lax.broadcasted_iota(i32, (rows, BS), 1).astype(f32)
    hot = jnp.where(column == seg, 1.0, 0.0)
    hot_t[...] = hot.T[0 : hot_t.shape[0]].astype(bf16)
    hot_b = hot.astype(bf16)
    lower = lax.broadcasted_iota(i32, (rows, rows), 0) > lax.broadcasted_iota(i32, (rows, rows), 1)
    before = jnp.dot(jnp.where(lower, 1.0, 0.0).astype(bf16), hot_b, preferred_element_type=f32)
    ones8 = jnp.ones((8, rows), bf16)
    count = jnp.dot(ones8, hot_b, preferred_element_type=f32)
    pairs = jnp.floor((count + 1.0) * 0.5)

    def group(e):
        total = jnp.zeros(e.shape, f32)
        for r in range(4):
            total = total + jnp.where(e >= BLK + r * RIM, 1.0, 0.0)
        return total

    e0 = lax.broadcasted_iota(i32, (BS, BS), 0)
    e1 = lax.broadcasted_iota(i32, (BS, BS), 1)
    earlier = jnp.where((e0 < e1) & (group(e0) == group(e1)), 1.0, 0.0).astype(bf16)
    e8 = lax.broadcasted_iota(i32, (8, BS), 1)
    g8 = group(e8)
    base = jnp.where(g8 > 0, OWN_PAIRS + (g8 - 1.0) * RIM_PAIRS, 0.0)
    start = jnp.dot(pairs.astype(bf16), earlier, preferred_element_type=f32) + base
    rank = jnp.sum(hot * before, axis=1, keepdims=True)
    first = jnp.sum(hot * (2.0 * start[0:1]), axis=1, keepdims=True)
    valid = column[:, 0:1] < 100.0
    pos = jnp.where(valid, rank + first, -1.0)
    place = lax.broadcasted_iota(i32, (rows, N_POS), 1).astype(f32)
    at = jnp.where(pos == place, 1.0, 0.0)
    entry = lax.broadcasted_iota(i32, (8, rows), 1)
    which = lax.broadcasted_iota(i32, (8, rows), 0)
    vals = jnp.where(which == 0, (entry & 31) + 1, jnp.where(which == 1, entry >> 5, 0)).astype(f32).astype(bf16)
    found = jnp.dot(vals, at.astype(bf16), preferred_element_type=f32)
    opens = jnp.dot(ones8, jnp.where(rank == 0.0, at, 0.0).astype(bf16), preferred_element_type=f32)
    b = found[0:1] - 1.0
    s = found[1:2]
    p = lax.broadcasted_iota(i32, (1, N_POS), 1)
    own_w = jnp.where(b < RIM_ROWS, b * K_IN + s, RIM_ROWS * K_IN + (b - RIM_ROWS) * K + s)
    rim_w = jnp.clip(b * (K - K_IN) + s - K_IN, 0.0, N_RIM - 1.0)
    w = jnp.where(p < OWN_POS, jnp.clip(own_w, 0.0, N_OWN - 1.0), rim_w)
    source = jnp.where(b >= 0, jnp.minimum(b, BLK - 1.0), float(BLK))
    end = start + pairs - 1.0
    end = jnp.where(g8 > 0, jnp.clip(end - OWN_PAIRS, 0.0, 4 * RIM_PAIRS - 1.0), jnp.clip(end, 0.0, OWN_PAIRS - 1.0))
    tab_i[0:1, :] = jnp.clip(w.astype(i32), 0, jnp.where(p < OWN_POS, N_OWN - 1, N_RIM - 1))
    tab_i[1:2, :] = jnp.clip(source.astype(i32), 0, BLK)
    limit = jnp.where(e8[0:1] >= BLK, 4 * RIM_PAIRS - 1, OWN_PAIRS - 1)
    tab_i[2:3, 0:BS] = jnp.clip(end[0:1].astype(i32), 0, limit)
    tab_f[0:1, :] = 1.0 - opens[0:1]
    tab_f[1:2, 0:BS] = jnp.where(count[0:1] > 0, 1.0, 0.0)


def kernel(
    pat_ref, start_hbm, w_hbm, solve_ref, cur,
    wo, wr, wto, wtr, u, rim, recv_v, recv_t, send_t, recv_d, send_d,
    prev, acc, inv, run_o, run_r, pack, ar1, ar2, ar3,
    sums, rowsum, recv_x, send_i, recv_i, tab, ftab, ptab, hot_t, start_ref, tab_i, tab_f, tab_p, padded,
    w_sem, t_sem, xs, xr, rs, rr, vs, vr, ts, tr, ds, dr, s1, r1, s2, r2, s3, r3,
):
    ni = lax.axis_index("narrow")
    wi = lax.axis_index("wide")
    n_narrow = lax.axis_size("narrow")
    n_wide = lax.axis_size("wide")
    north = lax.rem(ni + n_narrow - 1, n_narrow)
    south = lax.rem(ni + 1, n_narrow)
    west = lax.rem(wi + n_wide - 1, n_wide)
    east = lax.rem(wi + 1, n_wide)
    neighbours = ({"narrow": north}, {"narrow": south}, {"wide": west}, {"wide": east})
    has = (ni > 0, ni < n_narrow - 1, wi > 0, wi < n_wide - 1)
    wy = wi // Z_CHIPS
    wz = lax.rem(wi, Z_CHIPS)
    group1 = [{"narrow": lax.rem(ni + k, n_narrow)} for k in (4, 3, 5, 2, 6, 1, 7)]
    group2 = [{"wide": lax.rem(wi + k * Z_CHIPS, n_wide)} for k in (2, 1, 3)]
    group3 = [{"wide": wy * Z_CHIPS + lax.rem(wz + k, Z_CHIPS)} for k in (4, 3, 5, 2, 6, 1, 7)]

    barrier = pltpu.get_barrier_semaphore()
    greeted = [{"wide": west}, {"wide": east}] + group1 + group2 + group3
    for peer in greeted:
        pl.semaphore_signal(barrier, inc=1, device_id=peer, device_id_type=MESH)

    rim_copies = []
    for b in range(RIM_ROWS):
        n = K - K_IN
        rim_copies.append(pltpu.make_async_copy(
            w_hbm.at[pl.ds(b * K + K_IN, n)], wr.at[pl.ds(b * n, n)], w_sem.at[b]))
    own_copies = []
    for b in range(BLK):
        n = K_IN if b < RIM_ROWS else K
        own_copies.append(pltpu.make_async_copy(
            w_hbm.at[pl.ds(b * K, n)], wo.at[pl.ds(own_index(b), n)], w_sem.at[RIM_ROWS + b]))
    start_copy = pltpu.make_async_copy(start_hbm, start_ref, t_sem.at[3])
    for copy in rim_copies + [start_copy] + own_copies:
        copy.start()
    build_tables(pat_ref, tab_i, tab_f, tab_p, hot_t, padded)
    table_copies = [
        pltpu.make_async_copy(source, target, t_sem.at[k])
        for k, (source, target) in enumerate(((tab_i, tab), (tab_f, ftab), (tab_p, ptab)))
    ]
    for copy in table_copies:
        copy.start()

    for a in range(3):
        u[a, BLK] = jnp.zeros((NVEC, BS), bf16)
    sums[...] = jnp.zeros_like(sums)

    def pair_product(lhs, w, at):
        left = jnp.concatenate([lhs(tab[1, at]), lhs(tab[1, at + 1])], axis=1)
        right = jnp.concatenate([w[tab[0, at]], w[tab[0, at + 1]]], axis=0)
        return jnp.dot(left, right, preferred_element_type=f32)

    def rim_out(lhs, d, put):
        run = None
        for q in range(d * RIM_PAIRS, (d + 1) * RIM_PAIRS):
            at = OWN_POS + 2 * q
            part = pair_product(lhs, wr, at)
            run = part if run is None else run * ftab[0, at] + part
            run_r[q] = run
        for j in range(RIM):
            e = BLK + d * RIM + j
            put(d, j, (run_r[tab[2, e]] * ftab[1, e]).astype(bf16))

    def own_back(lhs):
        per = OWN_PAIRS // T_GROUPS

        def body(g, run):
            for q in range(per):
                at = g * per + q
                part = pair_product(lhs, wo, 2 * at)
                run = run * ftab[0, 2 * at] + part
                run_o[at] = run
            return run

        lax.fori_loop(0, T_GROUPS, body, jnp.zeros((NVEC, BS), f32))

    ones8 = jnp.ones((8, K * BS), bf16)

    def column_sums(w, first, n, b, s0):
        wide = jnp.concatenate([w[first + s] for s in range(n)], axis=1)
        total = jnp.dot(ones8[:, :BS], wide, preferred_element_type=f32)
        for s in range(n):
            at = (s0 + s) * NVEC + b
            sums[at : at + 1] = total[0:1, s * BS : (s + 1) * BS]

    def row_sums(wt, first, n):
        return jnp.dot(ones8[:, : n * BS], wt[first : first + n].reshape(n * BS, BS), preferred_element_type=f32)

    def grouped_sums():
        high = sums[...].astype(bf16)
        low = (sums[...] - high.astype(f32)).astype(bf16)
        return jnp.dot(hot_t[...], high, preferred_element_type=f32) + jnp.dot(
            hot_t[...], low, preferred_element_type=f32)

    for copy in rim_copies:
        copy.wait()
    m = K - K_IN
    for b in range(RIM_ROWS):
        for s in range(m):
            wtr[b * m + s] = wr[b * m + s].T
        column_sums(wr, b * m, m, b, K_IN)
    degree_copies = []
    start_copies = []

    def send_degree():
        start_copy.wait()
        out = grouped_sums()
        for d in range(4):
            at = BLK + d * RIM
            send_d[d, 0:RIM] = out[at : at + RIM].astype(bf16)
        pl.semaphore_wait(barrier, len(greeted))
        for d in (2, 3, 0, 1):
            copy = pltpu.make_async_remote_copy(
                send_d.at[d], recv_d.at[OPP[d]], ds.at[d], dr.at[OPP[d]],
                device_id=neighbours[d], device_id_type=MESH)
            copy.start()
            degree_copies.append(copy)
        for d in (2, 3, 0, 1):
            copy = pltpu.make_async_remote_copy(
                start_ref.at[:, pl.ds(d * RIM * BS, RIM * BS)], recv_x.at[OPP[d]], xs.at[d], xr.at[OPP[d]],
                device_id=neighbours[d], device_id_type=MESH)
            copy.start()
            start_copies.append(copy)

    def own_row_sums(b):
        total = row_sums(wto, own_index(b), K_IN if b < RIM_ROWS else K)
        if b < RIM_ROWS:
            total = total + jnp.where(has[b // RIM], row_sums(wtr, b * m, m), 0.0)
        rowsum[b : b + 1] = total[0:1]

    rowsum[...] = jnp.ones_like(rowsum)
    send_d[...] = jnp.zeros_like(send_d)
    send_i[...] = jnp.zeros_like(send_i)
    chunks = [range(c, c + CHUNK) for c in range(0, BLK, CHUNK)]
    for c, chunk in enumerate(chunks):
        for b in chunk:
            own_copies[b].wait()
        if c == SEND_AT:
            send_degree()
        for b in chunk:
            n = K_IN if b < RIM_ROWS else K
            for s in range(n):
                wto[own_index(b) + s] = wo[own_index(b) + s].T
            column_sums(wo, own_index(b), n, b, 0)
        if c > 0:
            for b in chunks[c - 1]:
                own_row_sums(b)
    for b in chunks[-1]:
        own_row_sums(b)
    back = grouped_sums()
    degree = rowsum[...] + back[0:NVEC]
    rowsum[...] = degree
    for b in range(BLK):
        x = start_ref[:, b * BS : (b + 1) * BS].astype(f32)
        cur[b] = x
        prev[b] = x
    for copy in degree_copies:
        copy.wait_recv()
    for d in range(4):
        at = d * RIM
        arrived = jnp.where(has[d], recv_d[d].astype(f32), 0.0)
        rowsum[at : at + RIM] = rowsum[at : at + RIM] + arrived[0:RIM]
    inv[...] = 1.0 / jnp.sqrt(0.5 * rowsum[...])
    for copy in table_copies:
        copy.wait()
    root_copies = []
    for d in (2, 3, 0, 1):
        send_i[d, 0:RIM] = inv[d * RIM : d * RIM + RIM]
    for d in (2, 3, 0, 1):
        copy = pltpu.make_async_remote_copy(
            send_i.at[d], recv_i.at[OPP[d]], rs.at[d], rr.at[OPP[d]],
            device_id=neighbours[d], device_id_type=MESH)
        copy.start()
        root_copies.append(copy)
    for b in range(BLK):
        u[0, b] = (inv[b : b + 1] * cur[b]).astype(bf16)
    for copy in degree_copies:
        copy.wait_send()
    def step(a, carry):
        copies = []
        for d in (2, 3, 0, 1):
            copies.append(pltpu.make_async_remote_copy(
                u.at[a, pl.ds(d * RIM, RIM)], recv_v.at[a, OPP[d]], vs.at[a, d], vr.at[a, OPP[d]],
                device_id=neighbours[d], device_id_type=MESH))

        @pl.when(a > 0)
        def _():
            for copy in copies:
                copy.start()

        def put_terms(d, j, value):
            send_t[a, d, j] = value

        term_copies = []
        for pair in ((2, 3), (0, 1)):
            for d in pair:
                rim_out(lambda k: u[a, k], d, put_terms)
            for d in pair:
                copy = pltpu.make_async_remote_copy(
                    send_t.at[a, d], recv_t.at[a, OPP[d]], ts.at[a, d], tr.at[a, OPP[d]],
                    device_id=neighbours[d], device_id_type=MESH)
                copy.start()
                term_copies.append(copy)
        own_back(lambda k: u[a, k])
        for b in range(BLK):
            n = K_IN if b < RIM_ROWS else K
            o = own_index(b)
            left = jnp.concatenate([u[a, ptab[b, s]] for s in range(n)], axis=1)
            ahead = jnp.dot(left, wto[o : o + n].reshape(n * BS, BS), preferred_element_type=f32)
            acc[b] = ahead + run_o[tab[2, b]]
        alpha = jnp.where(a == 0, 1.0, 2.0).astype(f32) / HALF
        beta = jnp.where(a == 0, 0.0, 1.0).astype(f32)
        nxt = lax.rem(a + 1, 3)

        def land(pair):
            mine = slice(0, 2) if pair == (2, 3) else slice(2, 4)

            @pl.when(a == 0)
            def _():
                for copy in start_copies[mine] + root_copies[mine]:
                    copy.wait()
                for d in pair:
                    for j in range(RIM):
                        x = recv_x[d, :, j * BS : (j + 1) * BS].astype(f32)
                        x = jnp.where(has[d], recv_i[d, j : j + 1] * x, 0.0)
                        rim[d * RIM + j] = x.astype(bf16)

            @pl.when(a > 0)
            def _():
                for copy in copies[mine]:
                    copy.wait()
                for d in pair:
                    for j in range(RIM):
                        rim[d * RIM + j] = jnp.where(has[d], recv_v[a, d, j], jnp.zeros((NVEC, BS), bf16))

            for d in pair:
                for b in range(d * RIM, (d + 1) * RIM):
                    left = jnp.concatenate(
                        [rim[jnp.minimum(ptab[b, K_IN + s], RIM_ROWS - 1)] for s in range(m)], axis=1)
                    acc[b] += jnp.dot(left, wtr[b * m : b * m + m].reshape(m * BS, BS), preferred_element_type=f32)

        def advance(blocks):
            for b in blocks:
                total = acc[b]
                if b < RIM_ROWS:
                    total = total + jnp.where(has[b // RIM], recv_t[a, b // RIM, b % RIM].astype(f32), 0.0)
                root = inv[b : b + 1]
                y = cur[b]
                new = alpha * ((y - (0.5 * root) * total) - CENTER * y) - beta * prev[b]
                prev[b] = y
                cur[b] = new
                u[nxt, b] = (root * new).astype(bf16)

        land((0, 1))
        land((2, 3))
        for copy in term_copies[2:]:
            copy.wait()
        advance(list(range(2 * RIM)) + list(range(RIM_ROWS, BLK)))
        for copy in term_copies[:2]:
            copy.wait()
        advance(range(2 * RIM, RIM_ROWS))
        return carry

    lax.fori_loop(0, 3, step, 0)

    highs = [cur[b].astype(bf16) for b in range(BLK)]
    lows = [(cur[b] - highs[b].astype(f32)).astype(bf16) for b in range(BLK)]
    stacked = jnp.concatenate([jnp.concatenate(highs, axis=1), jnp.concatenate(lows, axis=1)], axis=0)
    product = lax.dot_general(stacked, stacked, (((1,), (1,)), ((), ())), preferred_element_type=f32)
    gram = product[:NVEC, :NVEC] + product[NVEC:, NVEC:] + product[:NVEC, NVEC:] + product[NVEC:, :NVEC]
    packed = jnp.concatenate([gram[8 * g : 8 * g + 8] for g in range(4)], axis=1)

    for group, landing, sends, recvs in ((group1, ar1, s1, r1), (group2, ar2, s2, r2), (group3, ar3, s3, r3)):
        slot = {id(ar1): 0, id(ar2): 1, id(ar3): 2}[id(landing)]
        pack[slot] = packed
        sent = []
        for k, peer in enumerate(group):
            copy = pltpu.make_async_remote_copy(
                pack.at[slot], landing.at[k], sends.at[k], recvs.at[k],
                device_id=peer, device_id_type=MESH)
            copy.start()
            sent.append(copy)
        for copy in sent:
            copy.wait_recv()
        for k in range(len(group)):
            packed = packed + landing[k]
        for copy in sent:
            copy.wait_send()

    lane = lax.broadcasted_iota(i32, (NVEC, BS), 1)
    row = lax.broadcasted_iota(i32, (NVEC, BS), 0)
    moved = jnp.concatenate([pltpu.roll(packed, (96 - 32 * g) % 128, 1) for g in range(4)], axis=0)
    m = jnp.where(lane >= 96, moved, jnp.where(lax.rem(lane, 32) == row, 1.0, 0.0))
    roots = jnp.zeros((NVEC, BS), f32)
    for k in range(0, NVEC, 2):
        top = m[k : k + 1]
        low = m[k + 1 : k + 2]

        def spread(line, j):
            return jnp.broadcast_to(line[:, 96 + j : 97 + j], line.shape)

        d0 = spread(top, k)
        ratio = spread(top, k + 1) * (1.0 / d0)
        d1 = spread(low, k + 1) - spread(top, k + 1) * ratio
        second = low - ratio * top
        c0 = spread(m, k)
        c1 = spread(m, k + 1) - c0 * ratio
        roots = jnp.where(row == k, lax.rsqrt(d0), jnp.where(row == k + 1, lax.rsqrt(d1), roots))
        lower = m - c0 * (top * (1.0 / d0)) - c1 * (second * (1.0 / d1))
        m = jnp.where(row > k + 1, lower, jnp.where(row == k + 1, second, m))
    count = n_narrow * n_wide * BLK * BS
    solve = m * roots * math.sqrt(count)
    solve_ref[...] = solve


def last_kernel(solve_ref, y_ref, out_hbm, held, sem):
    solve = solve_ref[...]
    lane = lax.broadcasted_iota(i32, (NVEC, BS), 1)
    solve_high = solve.astype(bf16)
    solve_low = (solve - solve_high.astype(f32)).astype(bf16)
    left = jnp.where((lane >= 32) & (lane < 64), solve_low.astype(f32), solve_high.astype(f32))
    left = jnp.where(lane < 96, left, 0.0).astype(bf16)
    copies = []
    for c in range(OUT_PARTS):
        per = BLK // OUT_PARTS
        for b in range(c * per, (c + 1) * per):
            y = y_ref[b]
            high = y.astype(bf16)
            low = (y - high.astype(f32)).astype(bf16)
            right = jnp.concatenate([high, high, low, low], axis=0)
            held[:, b * BS : (b + 1) * BS] = jnp.dot(left, right, preferred_element_type=f32)
        part = pl.ds(c * per * BS, per * BS)
        copies.append(pltpu.make_async_copy(held.at[:, part], out_hbm.at[:, part], sem.at[c]))
        copies[-1].start()
    for copy in copies:
        copy.wait()


def body(start_block, weights, pattern):
    dma = pltpu.SemaphoreType.DMA
    vmem = pltpu.VMEM
    solve, final = pl.pallas_call(
        kernel,
        out_shape=[
            vmem((NVEC, BS), f32),
            vmem((BLK, NVEC, BS), f32),
        ],
        in_specs=[
            pl.BlockSpec(memory_space=pltpu.VMEM),
            pl.BlockSpec(memory_space=pl.ANY),
            pl.BlockSpec(memory_space=pl.ANY),
        ],
        out_specs=[pl.BlockSpec(memory_space=pltpu.VMEM)] * 2,
        scratch_shapes=[
            vmem((N_OWN, BS, BS), bf16),
            vmem((N_RIM, BS, BS), bf16),
            vmem((N_OWN, BS, BS), bf16),
            vmem((N_RIM, BS, BS), bf16),
            vmem((3, BLK + 1, NVEC, BS), bf16),
            vmem((RIM_ROWS, NVEC, BS), bf16),
            vmem((3, 4, RIM, NVEC, BS), bf16),
            vmem((3, 4, RIM, NVEC, BS), bf16),
            vmem((3, 4, RIM, NVEC, BS), bf16),
            vmem((4, 8, BS), bf16),
            vmem((4, 8, BS), bf16),
            vmem((BLK, NVEC, BS), f32),
            vmem((BLK, NVEC, BS), f32),
            vmem((NVEC, BS), f32),
            vmem((OWN_PAIRS, NVEC, BS), f32),
            vmem((4 * RIM_PAIRS, NVEC, BS), f32),
            vmem((3, 8, BS), f32),
            vmem((7, 8, BS), f32),
            vmem((3, 8, BS), f32),
            vmem((7, 8, BS), f32),
            vmem((K * NVEC, BS), f32),
            vmem((NVEC, BS), f32),
            vmem((4, NVEC, RIM * BS), bf16),
            vmem((4, 8, BS), f32),
            vmem((4, 8, BS), f32),
            pltpu.SMEM((8, N_POS), i32),
            pltpu.SMEM((8, N_POS), f32),
            pltpu.SMEM((NVEC, BS), i32),
            vmem((64, K * NVEC), bf16),
            vmem((NVEC, BLK * BS), bf16),
            vmem((8, N_POS), i32),
            vmem((8, N_POS), f32),
            vmem((NVEC, BS), i32),
            vmem((NVEC, BS), f32),
            dma((RIM_ROWS + BLK,)),
            dma((4,)),
            dma((4,)),
            dma((4,)),
            dma((4,)),
            dma((4,)),
            dma((3, 4)),
            dma((3, 4)),
            dma((3, 4)),
            dma((3, 4)),
            dma((4,)),
            dma((4,)),
            dma((7,)),
            dma((7,)),
            dma((3,)),
            dma((3,)),
            dma((7,)),
            dma((7,)),
        ],
        compiler_params=pltpu.CompilerParams(
            collective_id=0, has_side_effects=True, vmem_limit_bytes=56 * 2**20
        ),
        name="filter_step",
    )(jnp.transpose(pattern, (0, 3, 1, 2)).reshape(K, 1, BLK), start_block[0, 0], weights.reshape(BLK * K, BS, BS))
    out = pl.pallas_call(
        last_kernel,
        out_shape=jax.ShapeDtypeStruct((NVEC, BLK * BS), f32),
        in_specs=[pl.BlockSpec(memory_space=pltpu.VMEM)] * 2,
        out_specs=pl.BlockSpec(memory_space=pl.ANY),
        scratch_shapes=[vmem((NVEC, BLK * BS), f32), dma((OUT_PARTS,))],
        compiler_params=pltpu.CompilerParams(vmem_limit_bytes=8 * 2**20),
        name="last_product",
    )(solve, final)
    return out.reshape(1, 1, NVEC, BLK * BS)


def solution(mesh):
    placed = (
        P("narrow", "wide", None, None),
        P("narrow", "wide", None, None, None, None),
        P("narrow", "wide", None, None),
    )
    return jax.shard_map(
        body, mesh=mesh, in_specs=placed, out_specs=P("narrow", "wide", None, None), check_vma=False
    )
```
